32 devices in a mesh: rep: 2 (over x), idx: 16 (over z, y, core).
Axes of the slice: x: 2, y: 2, z: 4, core: 2. Of those that a mesh axis runs over, the one named last changes fastest.
Arguments:
- images: bfloat16 [16448, 1408], P(('rep', 'idx')), parts along dimension 0, may hold values from -6 to 6
- norm_gain: float32 [1408], replicated, may hold values from 0.25 to 1.75
- qkv_values: bfloat16 [1408, 4224], P(None, 'idx'), may hold values from -0.5 to 0.5
- qkv_exponents: int32 [11, 4224], replicated, may hold values from -2 to 2
- proj_values: bfloat16 [1408, 1408], P(None, 'idx'), may hold values from -0.078125 to 0.078125
- proj_exponents: int32 [11, 1408], replicated, may hold values from -2 to 2
- captions: bfloat16 [32768, 1408], P(('rep', 'idx')), parts along dimension 0, may hold values from -0.15625 to 0.15625
- owners: int32 [16448, 1], P(('rep', 'idx')), parts along dimension 0, may hold values from 0 to 15; in each aligned block of 514 rows (0 to 513, 514 to 1027, ...) at most 34 rows name the same one
- candidates: int32 [16448, 4], P(('rep', 'idx')), parts along dimension 0, may hold values from 0 to 7, all different within a row
Outputs:
- embedding: bfloat16 [16448, 1408], P(('rep', 'idx')), parts along dimension 0
- scores: bfloat16 [16448, 4, 128], P(('rep', 'idx')), parts along dimension 0
The draws below stay inside these ranges and needn't reach their ends.
There are 2 independent parts, one for each index of `rep`. The reference program is written for one: setup_inputs(seed, part) draws one part's arguments, and reference() takes and returns one part's arrays. A program takes and returns all parts, laid end to end along the dimension named above; an argument that names none is the same for every part. Nothing has to cross between parts.
Inputs may be any that keep to these rules, and one draw needn't show every extreme that they name: `owners`: among the tokens of one device no owner is named more than 34 times, a bound that some block reaches. `candidates`: each token names 4 different caption blocks.
All inputs are finite; a program needn't handle non-finite values.
Results may differ from the reference program's by a relative error of at most 0.004.
The reference program's roundings to bfloat16 on the way (of `normed`, `w_qkv`, `w_proj`, `qkv_rows`, `attn_probs` and `mixed_heads`) count: a program that leaves them out, or rounds other values in their place, can miss the bound.
Values may be sent and summed in bfloat16 or wider, within the bound.
A program may use at most 192 MiB of HBM per device.

```python
import math
import jax
import jax.numpy as jnp
import numpy as np
from jax import lax

D = 1408
HEADS = 16
PATCHES = 257
QBLK = 128
CBLK = 8
CAPT = 128
K = 4
TOK_DEV = 514
TOKENS = 8224
CAP = 34
CAPTIONS = 16384
N_IDX = 16


def draw_qkv_values(key, part):
    base_draw = jax.random.normal(jax.random.fold_in(key, 11), (D, 3 * D), jnp.float32) * (D * 4.26) ** (-0.5)
    return jnp.clip(base_draw, -0.5, 0.5).astype(jnp.bfloat16)


def place_ends(drawn, rng, low, largest):
    index_at = [jax.random.randint(jax.random.fold_in(rng, axis), (), 0, length) for axis, length in enumerate(drawn.shape)]
    main_axis = drawn.shape.index(max(drawn.shape))
    neighbour = index_at[:main_axis] + [(index_at[main_axis] + 1) % drawn.shape[main_axis]] + index_at[main_axis + 1:]
    return drawn.at[tuple(index_at)].set(low).at[tuple(neighbour)].set(largest)


def steps_of(rng, shape, pieces, low, top_value):
    loudness, own = 1.0, jax.random.fold_in(rng, 6)
    for dim, shards_of in pieces:
        steps = jnp.exp(jax.random.uniform(jax.random.fold_in(own, dim), (shards_of,), jnp.float32, low / len(pieces), top_value / len(pieces)))
        loudness = loudness * jnp.repeat(steps, shape[dim] // shards_of).reshape([-1 if axis == dim else 1 for axis in range(len(shape))])
    return loudness


def distinct(rng, rows, amount, top, lift):
    order = jax.random.permutation(jax.random.fold_in(rng, 1), amount)
    boost = order
    for power in range(3):
        boost = boost * boost // amount
    boost = boost * lift // amount
    tickets = jax.random.randint(jax.random.fold_in(rng, 2), (rows, amount), 0, 4096) + boost
    sure = jax.random.permutation(jax.random.fold_in(rng, 3), rows)[jnp.arange(amount) % rows]
    tickets = jnp.where(jnp.arange(rows)[:, None] == sure[None, :], 1 << 14, tickets)
    score = tickets * amount + jnp.arange(amount)
    return lax.top_k(score.astype(jnp.int32), top)[1].astype(jnp.int32)


def routed_block(key, own, number, rows, number_of, top, limit, lean):
    sequence = jax.random.permutation(key, number_of)
    packed, ordinary = portions_of(number_of, rows * top, limit, lean, True), portions_of(number_of, rows * top, limit, lean, False)
    places = jnp.arange(number_of)

    def named(lengths, rotation):
        used = int((lengths > 0).sum())
        fixed = max(1, used // 4)
        passed = fixed + (places - fixed + rotation * (used - fixed)) % max(1, number_of - fixed)
        return jnp.zeros((number_of,), jnp.int32).at[sequence[jnp.where(places < fixed, places, passed)]].set(jnp.asarray(lengths, jnp.int32))

    lengths = jnp.where(number % 4 == 0, named(packed, number // 4), named(ordinary, number - number // 4 - 1))
    mixed = jax.random.permutation(jax.random.fold_in(own, 3), number_of)
    donor, sink = mixed[0:number_of // 2 * 2:2], mixed[1:number_of // 2 * 2:2]
    room = jnp.minimum(lengths[donor] - 1, limit - lengths[sink]) // 2
    room = jnp.where((donor == sequence[0]) | (sink == sequence[0]) | (lengths[sink] == 0), 0, jnp.maximum(room, 0))
    passed = jax.random.randint(jax.random.fold_in(own, 4), (number_of // 2,), 0, 1 << 20) % (room + 1)
    lengths = lengths.at[donor].add(-passed).at[sink].add(passed)
    items = jnp.searchsorted(jnp.cumsum(lengths), jnp.arange(rows * top), side="right").astype(jnp.int32)
    grid = items.reshape(top, rows).T
    grid = grid[jax.random.permutation(jax.random.fold_in(own, 1), rows)]
    rotation = jax.random.randint(jax.random.fold_in(own, 2), (rows, 1), 0, top)
    return jnp.take_along_axis(grid, (jnp.arange(top)[None, :] + rotation) % top, axis=1)


def portions_of(amount, total, most, lean, full):
    loads = [(1 << 20) // math.isqrt(standing ** lean) + 1 for standing in range(1, amount + 1)]
    largest = most if full else min(most, max(-(-total // amount), total * loads[0] // sum(loads)))
    least = 1 if total - largest >= amount - 1 else 0
    holding, rest = [largest] + [least] * (amount - 1), total - largest - least * (amount - 1)
    while rest > 0:
        free = [i for i in range(1, amount) if holding[i] < largest] or [i for i in range(1, amount) if holding[i] < most]
        whole, budget = sum([loads[i] for i in free]), rest
        for i in free:
            addition = min(most - holding[i], max(1, budget * loads[i] // whole), rest)
            holding[i] = holding[i] + addition
            rest = rest - addition
    return np.array(holding)


def normal_values(rng, shape, scale, bound, split=(), kind=jnp.bfloat16):
    level = steps_of(rng, shape, split, -0.22, 0.18) if split else 1.0
    entries = jax.random.normal(rng, shape, jnp.float32) * scale * level
    return jnp.minimum(jnp.maximum(entries, -bound), bound).astype(kind)


def setup_inputs(seed: int = 0, part: int = 0) -> dict:
    streams_of = jax.random.split(jax.random.key(seed), 10)
    own_keys = jax.random.split(jax.random.fold_in(streams_of[9], part), 10)
    images = normal_values(own_keys[0], (TOKENS, D), 1.0, 6.0, ((0, 16),))
    norm_gain = jnp.clip(1.0 + 0.15 * jax.random.normal(streams_of[1], (D,), jnp.float32), 0.25, 1.75)
    qkv_values = draw_qkv_values(jax.random.fold_in(streams_of[9], 71), part)
    qkv_exponents = place_ends(jax.random.randint(streams_of[3], (D // QBLK, 3 * D), -2, 3), jax.random.fold_in(streams_of[3], 1), -2, 2).astype(jnp.int32)
    proj_values = normal_values(streams_of[4], (D, D), (4 * D) ** -0.5, 0.078125, ((1, 16),))
    proj_exponents = place_ends(jax.random.randint(streams_of[5], (D // QBLK, D), -2, 3), jax.random.fold_in(streams_of[5], 1), -2, 2).astype(jnp.int32)
    captions = normal_values(own_keys[6], (CAPTIONS, D), D ** -0.5, 0.15625, ((0, 16),))
    owners_keys = jax.random.split(jax.random.fold_in(own_keys[7], 1), TOKENS // TOK_DEV)
    owners_turns = jax.random.permutation(jax.random.fold_in(own_keys[7], 3), TOKENS // TOK_DEV)
    owners = jax.vmap(lambda own, number: routed_block(jax.random.fold_in(own_keys[7], 2), own, number, TOK_DEV, N_IDX, 1, CAP, 2))(owners_keys, owners_turns).reshape((TOKENS, 1))
    candidates = distinct(own_keys[8], TOKENS, CBLK, K, 4096)
    return dict(images=images, norm_gain=norm_gain, qkv_values=qkv_values, qkv_exponents=qkv_exponents, proj_values=proj_values, proj_exponents=proj_exponents, captions=captions, owners=owners, candidates=candidates)


def dequant(stored, exponents):
    row_count, col_count = stored.shape
    block_count = exponents.shape[0]
    scaled = stored.astype(jnp.float32).reshape(block_count, row_count // block_count, col_count)
    scaled = scaled * jnp.exp2(exponents.astype(jnp.float32))[:, None, :]
    return scaled.reshape(row_count, col_count).astype(jnp.bfloat16)

def layer_norm(token_rows, norm_gain):
    values = token_rows.astype(jnp.float32)
    centered = values - lax.optimization_barrier(jnp.mean(values, axis=-1, keepdims=True))
    inv_scale = lax.rsqrt(lax.optimization_barrier(jnp.mean(centered * centered, axis=-1, keepdims=True)) + 1e-06)
    return (centered * inv_scale * norm_gain.astype(jnp.float32)).astype(jnp.bfloat16)

def attend(qkv_rows):
    head_dim = D // HEADS
    grouped = qkv_rows.reshape(-1, PATCHES, 3, HEADS, head_dim).astype(jnp.float32)
    queries = grouped[:, :, 0]
    keys_all = grouped[:, :, 1]
    values_all = grouped[:, :, 2]
    logits = jnp.einsum('gqhd,gkhd->ghqk', queries, keys_all) * head_dim ** (-0.5)
    logits = logits - lax.optimization_barrier(jnp.max(logits, axis=-1, keepdims=True))
    weights = jnp.exp(logits)
    attn_probs = (weights / lax.optimization_barrier(jnp.sum(weights, axis=-1, keepdims=True))).astype(jnp.bfloat16)
    mixed_heads = jnp.einsum('ghqk,gkhd->gqhd', attn_probs.astype(jnp.float32), values_all)
    return mixed_heads.astype(jnp.bfloat16).reshape(-1, D)

def reference(images, norm_gain, qkv_values, qkv_exponents, proj_values, proj_exponents, captions, owners, candidates):
    w_qkv = dequant(qkv_values, qkv_exponents)
    w_proj = dequant(proj_values, proj_exponents)

    def layer_pass(token_rows):
        normed = layer_norm(token_rows, norm_gain)
        qkv_rows = jnp.dot(normed, w_qkv, preferred_element_type=jnp.float32).astype(jnp.bfloat16)
        mixed_heads = attend(qkv_rows)
        hidden = token_rows.astype(jnp.float32) + jnp.dot(mixed_heads, w_proj, preferred_element_type=jnp.float32)
        inv_scale = lax.rsqrt(lax.optimization_barrier(jnp.mean(hidden * hidden, axis=-1, keepdims=True)) + 1e-06)
        return (hidden * inv_scale).astype(jnp.bfloat16)
    embedding = lax.map(layer_pass, images.reshape(-1, PATCHES, D)).reshape(-1, D)
    blocks = captions.reshape(-1, CAPT, D)
    chosen = (owners[:, 0:1] * CBLK + candidates).astype(jnp.int32)

    def score_block(block_pair):
        token_rows, block_picks = block_pair
        picked = blocks[block_picks].astype(jnp.float32)
        return jnp.einsum('bd,bkjd->bkj', token_rows.astype(jnp.float32), picked).astype(jnp.bfloat16)
    scores = lax.map(score_block, (embedding.reshape(-1, 16, D), chosen.reshape(-1, 16, K)))
    return (embedding, scores.reshape(-1, K, CAPT))
```

```python
import math
import jax
import jax.numpy as jnp
from jax import lax
from jax.experimental import pallas as pl
from jax.experimental.pallas import tpu as pltpu
from jax.sharding import PartitionSpec as P

HEADS = 16
PATCHES = 257
CBLK = 8
CAPT = 128
F32 = jnp.float32
BF16 = jnp.bfloat16
VMEM = pltpu.VMEM
VLIMIT = 60 * 1024 * 1024


def dequant_rows(stored, exponents):
    row_count, col_count = stored.shape
    block_count = exponents.shape[0]
    turned = stored.T.astype(F32).reshape(col_count, block_count, row_count // block_count)
    scaled = turned * jnp.exp2(exponents.astype(F32)).T[:, :, None]
    return scaled.reshape(col_count, row_count).astype(BF16)


def layer_norm(token_rows, norm_gain):
    values = token_rows.astype(F32)
    centered = values - jnp.mean(values, axis=-1, keepdims=True)
    inv_scale = lax.rsqrt(jnp.mean(centered * centered, axis=-1, keepdims=True) + 1e-06)
    return (centered * inv_scale * norm_gain).astype(BF16)


def dot_nt(left, right):
    return lax.dot_general(left, right, (((1,), (1,)), ((), ())), preferred_element_type=F32)


MESH = pl.DeviceIdType.MESH

def spans_of(rows):
    third = rows // 24 * 8
    return (0, rows - 2 * third), (rows - 2 * third, third), (rows - third, third)


def front_kernel(
    images_ref, gain_ref, q_own, p_own, mixed_ref, p_out,
    q_all, normed, qkv, mixed, rz, ry, rx, rc, sz, sy, sx, sc, held,
):
    peers = q_all.shape[0]
    nz = peers // 4
    group, units, head_dim, patches = qkv.shape
    lanes = normed.shape[0] // group
    share = units // peers
    me = lax.axis_index("idx")
    x = lax.axis_index("rep")
    z, y, c = me // 4, (me // 2) % 2, me % 2
    own, out = (q_own, p_own), (q_all, p_out)

    def at(zz, yy, cc):
        return (zz * 2 + yy) * 2 + cc

    to_y, to_c, to_x = (x, at(z, 1 - y, c)), (x, at(z, y, 1 - c)), (1 - x, me)
    to_up, to_down = (x, me + 4), (x, me - 4)
    barrier = pltpu.get_barrier_semaphore()

    def greet(target):
        pl.semaphore_signal(barrier, inc=1, device_id=target, device_id_type=MESH)

    for target in (to_y, to_c, to_x):
        greet(target)

    @pl.when(z + 1 < nz)
    def _():
        greet(to_up)

    @pl.when(z > 0)
    def _():
        greet(to_down)

    greeted = 3 + jnp.where(z + 1 < nz, 1, 0) + jnp.where(z > 0, 1, 0)
    pl.semaphore_wait(barrier, greeted)

    def rows(a, k):
        spans = spans_of(own[a].shape[0])
        if k == 0:
            return pl.ds(*spans[0])
        if k == 3:
            return pl.ds(0, own[a].shape[0])
        side = x if k == 1 else 1 - x
        return pl.ds(pl.multiple_of(spans[1][0] + spans[1][1] * side, 8), spans[1][1])

    def copy(a, shard, k, mine, send, recv, target):
        span = rows(a, k)
        return pltpu.make_async_remote_copy(
            src_ref=own[a].at[span] if mine else out[a].at[shard, span],
            dst_ref=out[a].at[shard, span],
            send_sem=send,
            recv_sem=recv,
            device_id=target,
            device_id_type=MESH,
        )

    def pos(zz, yy):
        return zz * 2 + yy

    def up(a, zz, k, mine=False):
        return copy(a, at(zz, y, c), k, mine, sz.at[0, a, zz, k], rz.at[a, zz, k], to_up)

    def down(a, zz, k, mine=False):
        return copy(a, at(zz, y, c), k, mine, sz.at[1, a, zz, k], rz.at[a, zz, k], to_down)

    def across(a, zz, k, yy, mine=False):
        return copy(a, at(zz, yy, c), k, mine, sy.at[a, zz, k], ry.at[a, zz, k], to_y)

    def plane(a, zz, yy, k):
        return copy(a, at(zz, yy, c), k, False, sx.at[a, pos(zz, yy)], rx.at[a, pos(zz, yy)], to_x)

    def core(a, zz, yy, cc, k, mine=False):
        slot = 0 if k == 3 else k
        return copy(
            a, at(zz, yy, cc), k, mine, sc.at[a, pos(zz, yy), slot], rc.at[a, pos(zz, yy), slot], to_c
        )

    def each(distance, body):
        if distance == 0:
            body(z, 0)
            return

        @pl.when(z - distance >= 0)
        def _():
            body(z - distance, -1)

        @pl.when(z + distance < nz)
        def _():
            body(z + distance, 1)

    def start_own(a):
        for k in (1, 0):

            @pl.when(z + 1 < nz)
            def _():
                up(a, z, k, True).start()

            @pl.when(z > 0)
            def _():
                down(a, z, k, True).start()

            across(a, z, k, y, True).start()
        core(a, z, y, c, 3, True).start()
        pltpu.make_async_copy(own[a], out[a].at[me], held.at[a]).start()

    def chain_event(a, step):
        def body(zz, side):
            for k in (1, 0):
                up(a, zz, k).wait_recv()
                if side < 0:

                    @pl.when(z + 1 < nz)
                    def _():
                        up(a, zz, k).start()
                else:

                    @pl.when(z > 0)
                    def _():
                        down(a, zz, k).start()

                across(a, zz, k, y).start()
                if k == 1:
                    plane(a, zz, y, 1).start()
                core(a, zz, y, c, k).start()

        each(step, body)

    def across_event(a, distance):
        def body(zz, side):
            for k in (1, 0):
                across(a, zz, k, 1 - y).wait_recv()
                if k == 1:
                    plane(a, zz, 1 - y, 1).start()
                core(a, zz, 1 - y, c, k).start()

        each(distance, body)

    def plane_event(a, distance):
        def body(zz, side):
            if side != 0:
                plane(a, zz, y, 2).wait_recv()
                core(a, zz, y, c, 2).start()
            plane(a, zz, 1 - y, 2).wait_recv()
            core(a, zz, 1 - y, c, 2).start()

        each(distance, body)

    events = dict(chain=chain_event, across=across_event, plane=plane_event, own=lambda a, _: start_own(a))

    def run(listed):
        for kind, a, distance in listed:
            events[kind](a, distance)

    def nearest(place):
        found = z
        for zz in range(nz):
            order = sorted(range(nz), key=lambda other: (abs(other - zz), other))
            for turn in range(nz):
                hit = jnp.logical_and(z == zz, place == turn)
                found = jnp.where(hit, order[turn], found)
        return found

    def settle(a, zz):
        @pl.when(zz == z)
        def _():
            pltpu.make_async_copy(own[a], out[a].at[me], held.at[a]).wait()
            core(a, z, y, 1 - c, 3).wait_recv()
            for k in (1, 0, 2):
                core(a, z, 1 - y, 1 - c, k).wait_recv()

        @pl.when(zz != z)
        def _():
            for yy in (y, 1 - y):
                for k in (1, 0, 2):
                    core(a, zz, yy, 1 - c, k).wait_recv()

    def qkv_step(turn, _):
        zz = nearest(turn)
        for number, listed in enumerate(QKV_EVENTS):

            @pl.when(turn == number)
            def _():
                run(listed)

        settle(0, zz)

        def product(part, _):
            shard = zz * 4 + part
            every = dot_nt(q_all[shard], normed[...])
            for g in range(group):
                found = every[:, g * lanes:g * lanes + patches].reshape(share, head_dim, patches)
                qkv[g, pl.ds(shard * share, share)] = found.astype(BF16)
            return 0

        lax.fori_loop(0, 4, product, 0)
        return 0

    scale = head_dim ** (-0.5)
    bunch = 4
    rounds = HEADS // bunch

    def head_step(turn, _):
        for number, listed in enumerate(HEAD_EVENTS):

            @pl.when(turn == number)
            def _():
                run(listed)

        g = turn // rounds
        for b in range(bunch):
            h = (turn % rounds) * bunch + b
            queries, keys, vals = qkv[g, h], qkv[g, HEADS + h], qkv[g, 2 * HEADS + h]
            logits = lax.dot_general(
                keys, queries, (((0,), (0,)), ((), ())), preferred_element_type=F32
            )
            logits = logits * scale
            weights = jnp.exp(logits - jnp.max(logits, axis=0, keepdims=True))
            probs = weights * (1.0 / jnp.sum(weights, axis=0, keepdims=True))
            found = jnp.dot(vals, probs.astype(BF16), preferred_element_type=F32)
            mixed[g, pl.ds(pl.multiple_of(h * head_dim, 8), head_dim), :] = found
        return 0

    start_own(0)
    normed[...] = jnp.zeros_like(normed)
    for g in range(group):
        normed[g * lanes:g * lanes + patches] = layer_norm(
            images_ref[g * patches:(g + 1) * patches], gain_ref[...]
        )
    lax.fori_loop(0, nz, qkv_step, 0)
    lax.fori_loop(0, group * rounds, head_step, 0)
    run(LAST_EVENTS)
    for g in range(group):
        mixed_ref[g * patches:(g + 1) * patches] = mixed[g].T.astype(BF16)
    for zz in range(nz):
        settle(1, zz)

    for a in range(2):
        for distance in range(nz):

            def finish(zz, side):
                first = side == 0
                for k in (1, 0):
                    if side <= 0:

                        @pl.when(z + 1 < nz)
                        def _():
                            up(a, zz, k, first).wait_send()

                    if side >= 0:

                        @pl.when(z > 0)
                        def _():
                            down(a, zz, k, first).wait_send()

                    across(a, zz, k, y, first).wait_send()
                for yy, mine in ((y, first), (1 - y, False)):
                    if mine:
                        core(a, zz, yy, c, 3, True).wait_send()
                        continue
                    plane(a, zz, yy, 1).wait_send()
                    for k in (1, 0, 2):
                        core(a, zz, yy, c, k).wait_send()

            each(distance, finish)


QKV_EVENTS = (
    (("chain", 0, 1), ("own", 1, 0), ("across", 0, 0), ("plane", 0, 0)),
    (("chain", 0, 2), ("across", 0, 1), ("plane", 0, 1)),
    (("chain", 0, 3), ("across", 0, 2), ("chain", 1, 1), ("plane", 0, 2)),
    (("across", 0, 3), ("across", 1, 0), ("chain", 1, 2), ("plane", 0, 3)),
)
HEAD_EVENTS = (
    (("across", 1, 1), ("chain", 1, 3), ("plane", 1, 0)),
    (("across", 1, 2),),
    (("plane", 1, 1),),
    (("across", 1, 3),),
    (("plane", 1, 2),),
    (),
    (),
    (("plane", 1, 3),),
)
LAST_EVENTS = ()


def fits(images, q_own, p_own, peers, reps):
    tokens, width = images.shape
    rows_whole = all(own.shape[0] % 88 == 0 for own in (q_own, p_own))
    layout = peers == 4 * len(QKV_EVENTS) and reps == 2
    return layout and rows_whole and width == peers * p_own.shape[0] and tokens % PATCHES == 0


def front_call(images, gain, q_own, p_own, peers):
    tokens, width = images.shape
    group = tokens // PATCHES
    head_dim = width // HEADS
    lanes = -(-PATCHES // 128) * 128
    full = pl.BlockSpec(memory_space=VMEM)
    nz = peers // 4
    dma = pltpu.SemaphoreType.DMA
    return pl.pallas_call(
        front_kernel,
        in_specs=[full] * 4,
        out_specs=(full, pl.BlockSpec(memory_space=pl.ANY)),
        out_shape=(
            jax.ShapeDtypeStruct((tokens, width), BF16),
            jax.ShapeDtypeStruct((peers,) + p_own.shape, BF16),
        ),
        scratch_shapes=[
            pltpu.VMEM((peers,) + q_own.shape, BF16),
            pltpu.VMEM((group * lanes, width), BF16),
            pltpu.VMEM((group, 3 * HEADS, head_dim, PATCHES), BF16),
            pltpu.VMEM((group, width, PATCHES), F32),
            dma((2, nz, 2)),
            dma((2, nz, 2)),
            dma((2, 2 * nz)),
            dma((2, 2 * nz, 3)),
            dma((2, 2, nz, 2)),
            dma((2, nz, 2)),
            dma((2, 2 * nz)),
            dma((2, 2 * nz, 3)),
            dma((2,)),
        ],
        compiler_params=pltpu.CompilerParams(
            collective_id=0, has_side_effects=True, vmem_limit_bytes=VLIMIT
        ),
        name="front",
    )(images, gain, q_own, p_own)


def qkv_kernel(images_ref, gain_ref, w_ref, out_ref, normed):
    group, unit, head_dim = out_ref.shape[0], out_ref.shape[1], out_ref.shape[2]

    @pl.when(pl.program_id(0) == 0)
    def _():
        normed[...] = layer_norm(images_ref[...], gain_ref[...])

    patches = out_ref.shape[3]
    every = dot_nt(w_ref[...], normed[...])
    for g in range(group):
        rows = every[:, g * patches:(g + 1) * patches]
        out_ref[g] = rows.reshape(unit, head_dim, patches).astype(BF16)


def qkv_call(images, gain, w_rows):
    tokens, width = images.shape
    patches = PATCHES
    group = tokens // patches
    head_dim = width // HEADS
    units = w_rows.shape[0] // head_dim
    step = 4
    return pl.pallas_call(
        qkv_kernel,
        grid=(units // step,),
        in_specs=[
            pl.BlockSpec((tokens, width), lambda i: (0, 0)),
            pl.BlockSpec((1, width), lambda i: (0, 0)),
            pl.BlockSpec((step * head_dim, width), lambda i: (i, 0)),
        ],
        out_specs=pl.BlockSpec((group, step, head_dim, patches), lambda i: (0, i, 0, 0)),
        out_shape=jax.ShapeDtypeStruct((group, units, head_dim, patches), BF16),
        scratch_shapes=[pltpu.VMEM((tokens, width), BF16)],
        compiler_params=pltpu.CompilerParams(vmem_limit_bytes=VLIMIT),
        name="qkv",
    )(images, gain, w_rows)


def attend_kernel(qkv_ref, proj_ref, images_ref, slot_ref, emb_ref, send_ref, mixed):
    group, units, head_dim, patches = qkv_ref.shape
    width = HEADS * head_dim
    scale = head_dim ** (-0.5)
    for g in range(group):

        @pl.loop(0, HEADS, unroll=4)
        def _(h):
            queries, keys, vals = qkv_ref[g, h], qkv_ref[g, HEADS + h], qkv_ref[g, 2 * HEADS + h]
            logits = lax.dot_general(
                keys, queries, (((0,), (0,)), ((), ())), preferred_element_type=F32
            )
            logits = logits * scale
            weights = jnp.exp(logits - jnp.max(logits, axis=0, keepdims=True))
            probs = weights * (1.0 / jnp.sum(weights, axis=0, keepdims=True))
            out = jnp.dot(vals, probs.astype(BF16), preferred_element_type=F32)
            mixed[pl.ds(pl.multiple_of(h * head_dim, 8), head_dim), :] = out

        left = mixed[...].T.astype(BF16)
        hidden = images_ref[g * patches:(g + 1) * patches, :].astype(F32) + dot_nt(left, proj_ref[...])
        inv_scale = lax.rsqrt(jnp.mean(hidden * hidden, axis=-1, keepdims=True) + 1e-06)
        emb_ref[g * patches:(g + 1) * patches, :] = (hidden * inv_scale).astype(BF16)
    slots = math.prod(send_ref.shape[:-1])
    tokens = group * patches
    pick = lax.broadcasted_iota(jnp.int32, (slots, tokens), 0) == slot_ref[...]
    onehot = jnp.where(pick, 1.0, 0.0).astype(BF16)
    sent = jnp.dot(onehot, emb_ref[...], preferred_element_type=F32).astype(BF16)
    if len(send_ref.shape) == 2:
        send_ref[...] = sent
        return
    peers, capacity = send_ref.shape[0], send_ref.shape[1]
    for p in range(peers):
        send_ref[p] = sent[p * capacity:(p + 1) * capacity]


def attend_call(qkv, w_proj, images, slot_row, slot_shape):
    tokens, width = images.shape
    patches = qkv.shape[3]
    group = tokens // patches
    full = pl.BlockSpec(memory_space=VMEM)
    return pl.pallas_call(
        attend_kernel,
        in_specs=[full] * 4,
        out_specs=(full, full),
        out_shape=(
            jax.ShapeDtypeStruct((group * patches, width), BF16),
            jax.ShapeDtypeStruct(slot_shape + (width,), BF16),
        ),
        scratch_shapes=[pltpu.VMEM((width, patches), F32)],
        compiler_params=pltpu.CompilerParams(vmem_limit_bytes=VLIMIT),
        name="attend",
    )(qkv, w_proj, images, slot_row)


def score_kernel(rows_ref, picks_ref, captions_ref, out_ref):
    every = dot_nt(rows_ref[...], captions_ref[...]).astype(BF16)
    for k in range(picks_ref.shape[1]):
        pick = picks_ref[:, k:k + 1].astype(F32)
        chosen = jnp.zeros((every.shape[0], CAPT), F32)
        for b in range(CBLK):
            block = every[:, b * CAPT:(b + 1) * CAPT].astype(F32)
            chosen = jnp.where(pick == float(b), block, chosen)
        out_ref[:, k * CAPT:(k + 1) * CAPT] = chosen.astype(BF16)


def score_call(rows, picks, captions):
    full = pl.BlockSpec(memory_space=VMEM)
    return pl.pallas_call(
        score_kernel,
        in_specs=[full] * 3,
        out_specs=full,
        out_shape=jax.ShapeDtypeStruct((rows.shape[0], picks.shape[1] * CAPT), BF16),
        compiler_params=pltpu.CompilerParams(vmem_limit_bytes=VLIMIT),
        name="score",
    )(rows, picks, captions)


def capacity_of(tokens, peers):
    return (tokens + peers - 1) // peers + 1


def split_of(tokens, peers):
    capacity = capacity_of(tokens, peers)
    return capacity // 8 * 8, capacity % 8


def stride_of(capacity):
    return -(-capacity // 8) * 8


def back_kernel(
    mixed_ref, proj_ref, images_ref, slot_ref, picks_ref, captions_ref, emb_ref, out_ref,
    onehot, rows_out, rows_in, picks_in, chosen, got, columns, rest_columns, emb, total,
    wide, rest_out, rest_in, tall, tail_out, tail_in,
    rs, rr, ps, pr, bs, br, es, er, ts, tr, own_sem,
):
    peers = picks_ref.shape[0]
    tokens = slot_ref.shape[1]
    width = rows_out.shape[1]
    full, extra = split_of(tokens, peers)
    base, count = peers * full, peers * extra
    pick_count = out_ref.shape[1]
    nz, block = peers // 4, 4 * full
    me = lax.axis_index("idx")
    rep = lax.axis_index("rep")
    z = me // 4
    barrier = pltpu.get_barrier_semaphore()
    for step in range(1, peers):
        pl.semaphore_signal(
            barrier, inc=1, device_id=(rep, (me + step) % peers), device_id_type=MESH
        )

    def at(p):
        return pl.ds(pl.multiple_of(p * full, 8), full)

    def mover(src, dst, sends, recvs, flat):
        def move(p, home):
            return pltpu.make_async_remote_copy(
                src_ref=src.at[at(p) if flat else p],
                dst_ref=dst.at[at(home) if flat else home],
                send_sem=sends.at[p],
                recv_sem=recvs.at[home],
                device_id=(rep, p),
                device_id_type=MESH,
            )

        return move

    def keeper(src, dst, number, flat):
        here = at(me) if flat else me
        return pltpu.make_async_copy(src.at[here], dst.at[here], own_sem.at[number])

    moves = (
        (rows_out, rows_in, rs, rr, True),
        (picks_ref, picks_in, ps, pr, False),
        (chosen, got, bs, br, True),
        (rest_out, rest_in, es, er, False),
        (tail_out, tail_in, ts, tr, False),
    )
    rows_to, picks_to, back_to, rest_to, tail_to = [mover(*m) for m in moves]
    own_rows, own_picks, own_back, own_rest, own_tail = [
        keeper(m[0], m[1], number, m[4]) for number, m in enumerate(moves)
    ]
    keep = pltpu.make_async_copy(emb, emb_ref, own_sem.at[len(moves)])

    def farthest(place):
        found = z
        for zz in range(nz):
            order = sorted(
                range(nz), key=lambda other: (-abs(other - zz), (other < nz // 2) == (zz < nz // 2))
            )
            for turn in range(nz):
                found = jnp.where(jnp.logical_and(z == zz, place == turn), order[turn], found)
        return found

    def each(zz, local, remote):
        for part in range(4):
            p = zz * 4 + part

            @pl.when(p == me)
            def _():
                local()

            @pl.when(p != me)
            def _():
                remote(p)

    def each_plane(body):
        def step(turn, _):
            body(farthest(turn))
            return 0

        lax.fori_loop(0, nz, step, 0)

    pl.semaphore_wait(barrier, peers - 1)
    own_picks.start()
    for step in range(1, peers):
        picks_to((me + step) % peers, me).start()

    def embed(start, size):
        here = pl.ds(start, size)
        pick = lax.broadcasted_iota(jnp.int32, (size, tokens), 0) == slot_ref[...] - start
        onehot[here, :] = jnp.where(pick, 1.0, 0.0).astype(BF16)
        mine = onehot[here, :]
        left = jnp.dot(mine, mixed_ref[...], preferred_element_type=F32).astype(BF16)
        hidden = jnp.dot(mine, images_ref[...], preferred_element_type=F32) + dot_nt(left, proj_ref[...])
        inv_scale = lax.rsqrt(jnp.mean(hidden * hidden, axis=-1, keepdims=True) + 1e-06)
        return hidden * inv_scale

    def project(zz):
        start = pl.multiple_of(zz * block, block)
        rows_out[pl.ds(start, block), :] = embed(start, block).astype(BF16)
        each(zz, own_rows.start, lambda p: rows_to(p, me).start())

    each_plane(project)
    rest = embed(base, count)
    rows_out[base:base + count, :] = rest.astype(BF16)
    wide[...] = jnp.zeros_like(wide)
    tiles = width // 128
    for e in range(extra):
        for t in range(tiles):
            u = e * tiles + t
            wide[:, u % 8, u // 8 * 128:u // 8 * 128 + 128] = rest[
                e * peers:(e + 1) * peers, t * 128:(t + 1) * 128
            ]
    rest_out[...] = wide[...].astype(BF16)
    each_plane(lambda zz: each(zz, own_rest.start, lambda p: rest_to(p, me).start()))
    emb[...] = lax.dot_general(
        onehot[...], rows_out[...], (((0,), (0,)), ((), ())), preferred_element_type=F32
    ).astype(BF16)
    keep.start()

    def chosen_of(every, picks, k):
        pick = picks[:, k:k + 1]
        best = jnp.zeros((every.shape[0], CAPT), F32)
        for b in range(CBLK):
            best = jnp.where(pick == float(b), every[:, b * CAPT:(b + 1) * CAPT], best)
        return best

    def score(zz):
        here = pl.ds(pl.multiple_of(zz * block, block), block)

        def landed(p):
            picks_to(p, p).wait_recv()
            rows_to(p, p).wait_recv()

        def kept():
            own_picks.wait()
            own_rows.wait()

        each(zz, kept, landed)
        for part in range(4):
            p = zz * 4 + part
            turned = picks_in[p].astype(F32).T
            columns[part * full:(part + 1) * full] = turned[:full, :]
            for e in range(extra):
                rest_columns[pl.ds(e * peers + p, 1), :] = turned[full + e:full + e + 1, :]
        every = dot_nt(rows_in[here, :], captions_ref[...])
        for k in range(pick_count):
            chosen[here, k * CAPT:(k + 1) * CAPT] = chosen_of(every, columns, k).astype(BF16)
        each(zz, own_back.start, lambda p: back_to(p, me).start())

    each_plane(score)
    each_plane(lambda zz: each(zz, own_rest.wait, lambda p: rest_to(p, p).wait_recv()))
    wide[...] = rest_in[...].astype(F32)
    for e in range(extra):
        for t in range(tiles):
            u = e * tiles + t
            part = wide[:, u % 8, u // 8 * 128:u // 8 * 128 + 128]
            rows_in[base + e * peers:base + (e + 1) * peers, t * 128:(t + 1) * 128] = part.astype(BF16)
    every = dot_nt(rows_in[base:base + count, :], captions_ref[...])
    tall[...] = jnp.zeros_like(tall)
    for k in range(pick_count):
        best = chosen_of(every, rest_columns, k)
        for e in range(extra):
            tall[:, e * pick_count + k, :] = best[e * peers:(e + 1) * peers]
    tail_out[...] = tall[...].astype(BF16)
    each_plane(lambda zz: each(zz, own_tail.start, lambda p: tail_to(p, me).start()))
    total[...] = jnp.zeros_like(total)

    def give(here):
        total[...] += lax.dot_general(
            onehot[here, :], got[here, :], (((0,), (0,)), ((), ())), preferred_element_type=F32
        )

    def take(zz):
        each(zz, own_back.wait, lambda p: back_to(p, p).wait_recv())
        give(pl.ds(pl.multiple_of(zz * block, block), block))

    each_plane(take)
    each_plane(lambda zz: each(zz, own_tail.wait, lambda p: tail_to(p, p).wait_recv()))
    tall[...] = tail_in[...].astype(F32)
    for k in range(pick_count):
        for e in range(extra):
            got[base + e * peers:base + (e + 1) * peers, k * CAPT:(k + 1) * CAPT] = tall[
                :, e * pick_count + k, :
            ].astype(BF16)
    give(pl.ds(base, count))
    for k in range(pick_count):
        out_ref[:, k, :] = total[:, k * CAPT:(k + 1) * CAPT].astype(BF16)
    keep.wait()

    def sent(p):
        for move in (rows_to, picks_to, back_to, rest_to, tail_to):
            move(p, me).wait_send()

    each_plane(lambda zz: each(zz, lambda: None, sent))


def back_call(mixed, w_proj, images, slot_row, picks, captions, pick_count):
    tokens, width = images.shape
    peers = picks.shape[0]
    full_rows, extra = split_of(tokens, peers)
    slots = peers * (full_rows + extra)
    rest_shape = (peers, 8, -(-extra * (width // 128) // 8) * 128)
    tail_shape = (peers, -(-extra * pick_count // 8) * 8, CAPT)
    full = pl.BlockSpec(memory_space=VMEM)
    dma = pltpu.SemaphoreType.DMA
    return pl.pallas_call(
        back_kernel,
        in_specs=[full] * 6,
        out_specs=(pl.BlockSpec(memory_space=pl.ANY), full),
        out_shape=(
            jax.ShapeDtypeStruct((tokens, width), BF16),
            jax.ShapeDtypeStruct((tokens, pick_count, CAPT), BF16),
        ),
        scratch_shapes=[
            VMEM((slots, tokens), BF16),
            VMEM((slots, width), BF16),
            VMEM((slots, width), BF16),
            VMEM(picks.shape, BF16),
            VMEM((slots, pick_count * CAPT), BF16),
            VMEM((slots, pick_count * CAPT), BF16),
            VMEM((4 * full_rows, picks.shape[1]), F32),
            VMEM((peers * extra, picks.shape[1]), F32),
            VMEM((tokens, width), BF16),
            VMEM((tokens, pick_count * CAPT), F32),
            VMEM(rest_shape, F32),
            VMEM(rest_shape, BF16),
            VMEM(rest_shape, BF16),
            VMEM(tail_shape, F32),
            VMEM(tail_shape, BF16),
            VMEM(tail_shape, BF16),
        ]
        + [dma((peers,))] * 10
        + [dma((6,))],
        compiler_params=pltpu.CompilerParams(
            collective_id=1, has_side_effects=True, vmem_limit_bytes=VLIMIT
        ),
        name="back",
    )(mixed, w_proj, images, slot_row, picks, captions)


def return_kernel(slot_ref, rows_ref, out_ref, *packed):
    if packed:
        (flat,) = packed
        flat[...] = jnp.zeros_like(flat)
        stride = flat.shape[0] // rows_ref.shape[0]
        for p in range(rows_ref.shape[0]):
            flat[p * stride:p * stride + rows_ref.shape[1], :] = rows_ref[p]
        rows = flat[...]
    else:
        rows = rows_ref[...]
    tokens, slots = out_ref.shape[0], rows.shape[0]
    pick = lax.broadcasted_iota(jnp.int32, (tokens, slots), 1) == slot_ref[...]
    onehot = jnp.where(pick, 1.0, 0.0).astype(BF16)
    got = jnp.dot(onehot, rows, preferred_element_type=F32).astype(BF16)
    for k in range(out_ref.shape[1]):
        out_ref[:, k, :] = got[:, k * CAPT:(k + 1) * CAPT]


def return_call(slot_col, rows, pick_count):
    full = pl.BlockSpec(memory_space=VMEM)
    return pl.pallas_call(
        return_kernel,
        in_specs=[full] * 2,
        out_specs=full,
        out_shape=jax.ShapeDtypeStruct((slot_col.shape[0], pick_count, CAPT), BF16),
        scratch_shapes=[pltpu.VMEM((rows.shape[0] * stride_of(rows.shape[1]), rows.shape[2]), BF16)]
        if rows.ndim == 3
        else [],
        compiler_params=pltpu.CompilerParams(vmem_limit_bytes=VLIMIT),
        name="give_back",
    )(slot_col, rows)


def local(
    images,
    norm_gain,
    qkv_values,
    qkv_exponents,
    proj_values,
    proj_exponents,
    captions,
    owners,
    candidates,
):
    token_count, width = images.shape
    peer_count = lax.axis_size("idx")
    me = lax.axis_index("idx")
    capacity = capacity_of(token_count, peer_count)

    def own_exponents(exponents, cols):
        return lax.dynamic_slice_in_dim(exponents, me * cols, cols, axis=1)

    qkv_cols, proj_cols = qkv_values.shape[1], proj_values.shape[1]
    qkv_own = dequant_rows(qkv_values, own_exponents(qkv_exponents, qkv_cols))
    proj_own = dequant_rows(proj_values, own_exponents(proj_exponents, proj_cols))
    joined = fits(images, qkv_own, proj_own, peer_count, lax.axis_size("rep"))

    owner_ids = owners[:, 0]
    onehot = (owner_ids[:, None] == jnp.arange(peer_count, dtype=jnp.int32)[None, :]).astype(
        jnp.int32
    )
    slot_rank = jnp.sum((jnp.cumsum(onehot, axis=0) - onehot) * onehot, axis=1)
    stride = stride_of(capacity) if joined else capacity
    slot_index = owner_ids * stride + slot_rank
    slots = peer_count * stride
    pick_count = candidates.shape[1]
    dispatch = (jnp.arange(slots, dtype=jnp.int32)[:, None] == slot_index[None, :]).astype(BF16)
    send_picks = jnp.dot(dispatch, candidates.astype(BF16), preferred_element_type=F32).astype(BF16)
    gain = norm_gain[None, :]
    if joined:
        turned = send_picks.reshape(peer_count, stride, pick_count).transpose(0, 2, 1)
        turned = jnp.pad(turned, ((0, 0), (0, 8 - pick_count), (0, 128 - stride)))
        whole, _ = split_of(token_count, peer_count)
        place = jnp.where(
            slot_rank < whole,
            owner_ids * whole + slot_rank,
            peer_count * slot_rank + owner_ids,
        )
        mixed, w_proj = front_call(images, gain, qkv_own, proj_own, peer_count)
        return back_call(
            mixed, w_proj.reshape(width, width), images, place[None, :], turned, captions, pick_count
        )
    w_qkv, w_proj = (lax.all_gather(own, "idx", axis=0, tiled=True) for own in (qkv_own, proj_own))
    qkv = qkv_call(images, gain, w_qkv)
    embedding, send_rows = attend_call(qkv, w_proj, images, slot_index[None, :], (slots,))

    def swap(blocks):
        shaped = blocks.reshape(peer_count, capacity, blocks.shape[1])
        moved = lax.all_to_all(shaped, "idx", split_axis=0, concat_axis=0, tiled=True)
        return moved.reshape(blocks.shape)

    returned = swap(score_call(swap(send_rows), swap(send_picks), captions))
    return (embedding, return_call(slot_index[:, None], returned, pick_count))


def solution(mesh):
    placed = (
        P(("rep", "idx"), None),
        P(),
        P(None, "idx"),
        P(),
        P(None, "idx"),
        P(),
        P(("rep", "idx"), None),
        P(("rep", "idx"), None),
        P(("rep", "idx"), None),
    )
    return jax.shard_map(
        local,
        mesh=mesh,
        in_specs=placed,
        out_specs=(P(("rep", "idx"), None), P(("rep", "idx"), None, None)),
        check_vma=False,
    )
```

```python
import math
import jax
import jax.numpy as jnp
from jax import lax
from jax.experimental import pallas as pl
from jax.experimental.pallas import tpu as pltpu
from jax.sharding import PartitionSpec as P

HEADS = 16
PATCHES = 257
CBLK = 8
CAPT = 128
F32 = jnp.float32
BF16 = jnp.bfloat16
VMEM = pltpu.VMEM
VLIMIT = 60 * 1024 * 1024


def dequant_rows(stored, exponents):
    row_count, col_count = stored.shape
    block_count = exponents.shape[0]
    turned = stored.T.astype(F32).reshape(col_count, block_count, row_count // block_count)
    scaled = turned * jnp.exp2(exponents.astype(F32)).T[:, :, None]
    return scaled.reshape(col_count, row_count).astype(BF16)


def layer_norm(token_rows, norm_gain):
    values = token_rows.astype(F32)
    centered = values - jnp.mean(values, axis=-1, keepdims=True)
    inv_scale = lax.rsqrt(jnp.mean(centered * centered, axis=-1, keepdims=True) + 1e-06)
    return (centered * inv_scale * norm_gain).astype(BF16)


def dot_nt(left, right):
    return lax.dot_general(left, right, (((1,), (1,)), ((), ())), preferred_element_type=F32)


MESH = pl.DeviceIdType.MESH

FRONT_LIMIT = 38 * 1024 * 1024
BACK_LIMIT = 40 * 1024 * 1024


def spans_of(rows):
    third = rows // 24 * 8
    return (0, rows - 2 * third), (rows - 2 * third, third), (rows - third, third)


def front_kernel(
    images_ref, gain_ref, q_own, p_own, mixed_ref, p_out,
    q_all, normed, qkv, mixed, rz, ry, rx, rc, sz, sy, sx, sc, held,
):
    peers = q_all.shape[0]
    nz = peers // 4
    group, units, head_dim, patches = qkv.shape
    lanes = normed.shape[0] // group
    share = units // peers
    me = lax.axis_index("idx")
    x = lax.axis_index("rep")
    z, y, c = me // 4, (me // 2) % 2, me % 2
    own, out = (q_own, p_own), (q_all, p_out)

    def at(zz, yy, cc):
        return (zz * 2 + yy) * 2 + cc

    to_y, to_c, to_x = (x, at(z, 1 - y, c)), (x, at(z, y, 1 - c)), (1 - x, me)
    to_up, to_down = (x, me + 4), (x, me - 4)
    barrier = pltpu.get_barrier_semaphore()

    def greet(target):
        pl.semaphore_signal(barrier, inc=1, device_id=target, device_id_type=MESH)

    for target in (to_y, to_c, to_x):
        greet(target)

    @pl.when(z + 1 < nz)
    def _():
        greet(to_up)

    @pl.when(z > 0)
    def _():
        greet(to_down)

    greeted = 3 + jnp.where(z + 1 < nz, 1, 0) + jnp.where(z > 0, 1, 0)
    pl.semaphore_wait(barrier, greeted)

    def rows(a, k):
        spans = spans_of(own[a].shape[0])
        if k == 0:
            return pl.ds(*spans[0])
        if k == 3:
            return pl.ds(0, own[a].shape[0])
        side = x if k == 1 else 1 - x
        return pl.ds(pl.multiple_of(spans[1][0] + spans[1][1] * side, 8), spans[1][1])

    def copy(a, shard, k, mine, send, recv, target):
        span = rows(a, k)
        return pltpu.make_async_remote_copy(
            src_ref=own[a].at[span] if mine else out[a].at[shard, span],
            dst_ref=out[a].at[shard, span],
            send_sem=send,
            recv_sem=recv,
            device_id=target,
            device_id_type=MESH,
        )

    def pos(zz, yy):
        return zz * 2 + yy

    def up(a, zz, k, mine=False):
        return copy(a, at(zz, y, c), k, mine, sz.at[0, a, zz, k], rz.at[a, zz, k], to_up)

    def down(a, zz, k, mine=False):
        return copy(a, at(zz, y, c), k, mine, sz.at[1, a, zz, k], rz.at[a, zz, k], to_down)

    def across(a, zz, k, yy, mine=False):
        return copy(a, at(zz, yy, c), k, mine, sy.at[a, zz, k], ry.at[a, zz, k], to_y)

    def plane(a, zz, yy, k):
        return copy(a, at(zz, yy, c), k, False, sx.at[a, pos(zz, yy)], rx.at[a, pos(zz, yy)], to_x)

    def core(a, zz, yy, cc, k, mine=False):
        slot = 0 if k == 3 else k
        return copy(
            a, at(zz, yy, cc), k, mine, sc.at[a, pos(zz, yy), slot], rc.at[a, pos(zz, yy), slot], to_c
        )

    def each(distance, body):
        if distance == 0:
            body(z, 0)
            return

        @pl.when(z - distance >= 0)
        def _():
            body(z - distance, -1)

        @pl.when(z + distance < nz)
        def _():
            body(z + distance, 1)

    def start_own(a):
        for k in (1, 0):

            @pl.when(z + 1 < nz)
            def _():
                up(a, z, k, True).start()

            @pl.when(z > 0)
            def _():
                down(a, z, k, True).start()

            across(a, z, k, y, True).start()
        core(a, z, y, c, 3, True).start()
        pltpu.make_async_copy(own[a], out[a].at[me], held.at[a]).start()

    def chain_event(a, step, kinds):
        def body(zz, side):
            for k in kinds:
                up(a, zz, k).wait_recv()
                if side < 0:

                    @pl.when(z + 1 < nz)
                    def _():
                        up(a, zz, k).start()
                else:

                    @pl.when(z > 0)
                    def _():
                        down(a, zz, k).start()

                across(a, zz, k, y).start()
                if k == 1:
                    plane(a, zz, y, 1).start()
                core(a, zz, y, c, k).start()

        each(step, body)

    def across_event(a, distance, kinds):
        def body(zz, side):
            for k in kinds:
                across(a, zz, k, 1 - y).wait_recv()
                if k == 1:
                    plane(a, zz, 1 - y, 1).start()
                core(a, zz, 1 - y, c, k).start()

        each(distance, body)

    def plane_event(a, distance):
        def body(zz, side):
            if side != 0:
                plane(a, zz, y, 2).wait_recv()
                core(a, zz, y, c, 2).start()
            plane(a, zz, 1 - y, 2).wait_recv()
            core(a, zz, 1 - y, c, 2).start()

        each(distance, body)

    def run(listed):
        for event in listed:
            a = int(event[-1] if event[0] == "o" else event[1])
            if event[0] == "o":
                start_own(a)
                continue
            distance, kinds = int(event[2]), tuple(int(k) for k in event[3:])
            if event[0] == "c":
                chain_event(a, distance, kinds)
            elif event[0] == "x":
                across_event(a, distance, kinds)
            else:
                plane_event(a, distance)

    def nearest(place):
        found = z
        for zz in range(nz):
            order = sorted(range(nz), key=lambda other: (abs(other - zz), other))
            for turn in range(nz):
                hit = jnp.logical_and(z == zz, place == turn)
                found = jnp.where(hit, order[turn], found)
        return found

    def settle(a, zz):
        @pl.when(zz == z)
        def _():
            pltpu.make_async_copy(own[a], out[a].at[me], held.at[a]).wait()
            core(a, z, y, 1 - c, 3).wait_recv()
            for k in (1, 0, 2):
                core(a, z, 1 - y, 1 - c, k).wait_recv()

        @pl.when(zz != z)
        def _():
            for yy in (y, 1 - y):
                for k in (1, 0, 2):
                    core(a, zz, yy, 1 - c, k).wait_recv()

    def qkv_step(turn, _):
        zz = nearest(turn // 4)
        for number, listed in enumerate(QKV_EVENTS):
            if listed:

                @pl.when(turn == number)
                def _():
                    run(listed)

        @pl.when(turn % 4 == 0)
        def _():
            settle(0, zz)

        shard = zz * 4 + turn % 4
        every = dot_nt(q_all[shard], normed[...])
        for g in range(group):
            found = every[:, g * lanes:g * lanes + patches].reshape(share, head_dim, patches)
            qkv[g, pl.ds(shard * share, share)] = found.astype(BF16)
        return 0

    scale = head_dim ** (-0.5)
    bunch = 4
    rounds = HEADS // bunch

    def head_step(turn, _):
        for number, listed in enumerate(HEAD_EVENTS):
            if listed:

                @pl.when(turn == number)
                def _():
                    run(listed)

        g = turn // rounds
        for b in range(bunch):
            h = (turn % rounds) * bunch + b
            queries, keys, vals = qkv[g, h], qkv[g, HEADS + h], qkv[g, 2 * HEADS + h]
            logits = lax.dot_general(
                keys, queries, (((0,), (0,)), ((), ())), preferred_element_type=F32
            )
            logits = logits * scale
            weights = jnp.exp(logits - jnp.max(logits, axis=0, keepdims=True))
            probs = weights * (1.0 / jnp.sum(weights, axis=0, keepdims=True))
            found = jnp.dot(vals, probs.astype(BF16), preferred_element_type=F32)
            mixed[pl.ds(pl.multiple_of(h * head_dim, 8), head_dim), :] = found
        for image in range(group):

            @pl.when(turn == image * rounds + rounds - 1)
            def _():
                mixed_ref[image * patches:(image + 1) * patches] = mixed[...].T.astype(BF16)

        return 0

    run(LEAD_EVENTS)
    normed[...] = jnp.zeros_like(normed)
    for g in range(group):
        normed[g * lanes:g * lanes + patches] = layer_norm(
            images_ref[g * patches:(g + 1) * patches], gain_ref[...]
        )
    lax.fori_loop(0, len(QKV_EVENTS), qkv_step, 0)
    lax.fori_loop(0, group * rounds, head_step, 0)
    run(LAST_EVENTS)
    for zz in range(nz):
        settle(1, zz)

    for a in range(2):
        for distance in range(nz):

            def finish(zz, side):
                first = side == 0
                for k in (1, 0):
                    if side <= 0:

                        @pl.when(z + 1 < nz)
                        def _():
                            up(a, zz, k, first).wait_send()

                    if side >= 0:

                        @pl.when(z > 0)
                        def _():
                            down(a, zz, k, first).wait_send()

                    across(a, zz, k, y, first).wait_send()
                for yy, mine in ((y, first), (1 - y, False)):
                    if mine:
                        core(a, zz, yy, c, 3, True).wait_send()
                        continue
                    plane(a, zz, yy, 1).wait_send()
                    for k in (1, 0, 2):
                        core(a, zz, yy, c, k).wait_send()

            each(distance, finish)


LEAD_EVENTS = ("own0", "x001", "c011",)
QKV_EVENTS = (
    ("x000", "c010", "x011", "p00", "c021", "c020",),
    (),
    ("c031",),
    ("own1", "x010",),
    ("p01", "x021",),
    (),
    ("c030", "x031", "c111",),
    ("x020",),
    ("p02", "c121", "x101",),
    ("c110", "p03",),
    ("x030",),
    (),
    (),
    ("c131",),
    ("c120",),
    (),
)
HEAD_EVENTS = (
    (),
    ("c130",),
    ("p10", "x121", "x131", "x111",),
    (),
    (),
    ("p13", "x120", "p12",),
    ("p11", "x100", "x110", "x130",),
    (),
)
LAST_EVENTS = ()


def fits(images, q_own, p_own, peers, reps):
    tokens, width = images.shape
    rows_whole = all(own.shape[0] % 88 == 0 for own in (q_own, p_own))
    layout = peers == len(QKV_EVENTS) and reps == 2
    return layout and rows_whole and width == peers * p_own.shape[0] and tokens % PATCHES == 0


def front_call(images, gain, q_own, p_own, peers):
    tokens, width = images.shape
    group = tokens // PATCHES
    head_dim = width // HEADS
    lanes = -(-PATCHES // 128) * 128
    full = pl.BlockSpec(memory_space=VMEM)
    nz = peers // 4
    dma = pltpu.SemaphoreType.DMA
    return pl.pallas_call(
        front_kernel,
        in_specs=[full] * 4,
        out_specs=(full, pl.BlockSpec(memory_space=pl.ANY)),
        out_shape=(
            jax.ShapeDtypeStruct((tokens, width), BF16),
            jax.ShapeDtypeStruct((peers,) + p_own.shape, BF16),
        ),
        scratch_shapes=[
            pltpu.VMEM((peers,) + q_own.shape, BF16),
            pltpu.VMEM((group * lanes, width), BF16),
            pltpu.VMEM((group, 3 * HEADS, head_dim, PATCHES), BF16),
            pltpu.VMEM((width, PATCHES), F32),
            dma((2, nz, 2)),
            dma((2, nz, 2)),
            dma((2, 2 * nz)),
            dma((2, 2 * nz, 3)),
            dma((2, 2, nz, 2)),
            dma((2, nz, 2)),
            dma((2, 2 * nz)),
            dma((2, 2 * nz, 3)),
            dma((2,)),
        ],
        compiler_params=pltpu.CompilerParams(
            collective_id=0, has_side_effects=True, vmem_limit_bytes=FRONT_LIMIT
        ),
        name="front",
    )(images, gain, q_own, p_own)


def qkv_kernel(images_ref, gain_ref, w_ref, out_ref, normed):
    group, unit, head_dim = out_ref.shape[0], out_ref.shape[1], out_ref.shape[2]

    @pl.when(pl.program_id(0) == 0)
    def _():
        normed[...] = layer_norm(images_ref[...], gain_ref[...])

    patches = out_ref.shape[3]
    every = dot_nt(w_ref[...], normed[...])
    for g in range(group):
        rows = every[:, g * patches:(g + 1) * patches]
        out_ref[g] = rows.reshape(unit, head_dim, patches).astype(BF16)


def qkv_call(images, gain, w_rows):
    tokens, width = images.shape
    patches = PATCHES
    group = tokens // patches
    head_dim = width // HEADS
    units = w_rows.shape[0] // head_dim
    step = 4
    return pl.pallas_call(
        qkv_kernel,
        grid=(units // step,),
        in_specs=[
            pl.BlockSpec((tokens, width), lambda i: (0, 0)),
            pl.BlockSpec((1, width), lambda i: (0, 0)),
            pl.BlockSpec((step * head_dim, width), lambda i: (i, 0)),
        ],
        out_specs=pl.BlockSpec((group, step, head_dim, patches), lambda i: (0, i, 0, 0)),
        out_shape=jax.ShapeDtypeStruct((group, units, head_dim, patches), BF16),
        scratch_shapes=[pltpu.VMEM((tokens, width), BF16)],
        compiler_params=pltpu.CompilerParams(vmem_limit_bytes=VLIMIT),
        name="qkv",
    )(images, gain, w_rows)


def attend_kernel(qkv_ref, proj_ref, images_ref, slot_ref, emb_ref, send_ref, mixed):
    group, units, head_dim, patches = qkv_ref.shape
    width = HEADS * head_dim
    scale = head_dim ** (-0.5)
    for g in range(group):

        @pl.loop(0, HEADS, unroll=4)
        def _(h):
            queries, keys, vals = qkv_ref[g, h], qkv_ref[g, HEADS + h], qkv_ref[g, 2 * HEADS + h]
            logits = lax.dot_general(
                keys, queries, (((0,), (0,)), ((), ())), preferred_element_type=F32
            )
            logits = logits * scale
            weights = jnp.exp(logits - jnp.max(logits, axis=0, keepdims=True))
            probs = weights * (1.0 / jnp.sum(weights, axis=0, keepdims=True))
            out = jnp.dot(vals, probs.astype(BF16), preferred_element_type=F32)
            mixed[pl.ds(pl.multiple_of(h * head_dim, 8), head_dim), :] = out

        left = mixed[...].T.astype(BF16)
        hidden = images_ref[g * patches:(g + 1) * patches, :].astype(F32) + dot_nt(left, proj_ref[...])
        inv_scale = lax.rsqrt(jnp.mean(hidden * hidden, axis=-1, keepdims=True) + 1e-06)
        emb_ref[g * patches:(g + 1) * patches, :] = (hidden * inv_scale).astype(BF16)
    slots = math.prod(send_ref.shape[:-1])
    tokens = group * patches
    pick = lax.broadcasted_iota(jnp.int32, (slots, tokens), 0) == slot_ref[...]
    onehot = jnp.where(pick, 1.0, 0.0).astype(BF16)
    sent = jnp.dot(onehot, emb_ref[...], preferred_element_type=F32).astype(BF16)
    if len(send_ref.shape) == 2:
        send_ref[...] = sent
        return
    peers, capacity = send_ref.shape[0], send_ref.shape[1]
    for p in range(peers):
        send_ref[p] = sent[p * capacity:(p + 1) * capacity]


def attend_call(qkv, w_proj, images, slot_row, slot_shape):
    tokens, width = images.shape
    patches = qkv.shape[3]
    group = tokens // patches
    full = pl.BlockSpec(memory_space=VMEM)
    return pl.pallas_call(
        attend_kernel,
        in_specs=[full] * 4,
        out_specs=(full, full),
        out_shape=(
            jax.ShapeDtypeStruct((group * patches, width), BF16),
            jax.ShapeDtypeStruct(slot_shape + (width,), BF16),
        ),
        scratch_shapes=[pltpu.VMEM((width, patches), F32)],
        compiler_params=pltpu.CompilerParams(vmem_limit_bytes=VLIMIT),
        name="attend",
    )(qkv, w_proj, images, slot_row)


def score_kernel(rows_ref, picks_ref, captions_ref, out_ref):
    every = dot_nt(rows_ref[...], captions_ref[...]).astype(BF16)
    for k in range(picks_ref.shape[1]):
        pick = picks_ref[:, k:k + 1].astype(F32)
        chosen = jnp.zeros((every.shape[0], CAPT), F32)
        for b in range(CBLK):
            block = every[:, b * CAPT:(b + 1) * CAPT].astype(F32)
            chosen = jnp.where(pick == float(b), block, chosen)
        out_ref[:, k * CAPT:(k + 1) * CAPT] = chosen.astype(BF16)


def score_call(rows, picks, captions):
    full = pl.BlockSpec(memory_space=VMEM)
    return pl.pallas_call(
        score_kernel,
        in_specs=[full] * 3,
        out_specs=full,
        out_shape=jax.ShapeDtypeStruct((rows.shape[0], picks.shape[1] * CAPT), BF16),
        compiler_params=pltpu.CompilerParams(vmem_limit_bytes=VLIMIT),
        name="score",
    )(rows, picks, captions)


def capacity_of(tokens, peers):
    return (tokens + peers - 1) // peers + 1


def split_of(tokens, peers):
    capacity = capacity_of(tokens, peers)
    return capacity // 8 * 8, capacity % 8


def stride_of(capacity):
    return -(-capacity // 8) * 8


def back_kernel(
    mixed_far, proj_far, images_far, slot_ref, picks_ref, captions_far, emb_ref, out_ref,
    mixed_ref, proj_ref, images_ref, captions_ref, loads,
    onehot, rows_out, rows_in, picks_in, chosen, got, columns, rest_columns, emb, total,
    wide, rest_out, rest_in, tall, tail_out, tail_in,
    rs, rr, ps, pr, bs, br, es, er, ts, tr, own_sem,
):
    peers = picks_ref.shape[0]
    tokens = slot_ref.shape[1]
    width = rows_out.shape[1]
    full, extra = split_of(tokens, peers)
    base, count = peers * full, peers * extra
    pick_count = out_ref.shape[1]
    nz, block = peers // 4, 4 * full
    me = lax.axis_index("idx")
    rep = lax.axis_index("rep")
    z = me // 4
    barrier = pltpu.get_barrier_semaphore()
    for step in range(1, peers):
        pl.semaphore_signal(
            barrier, inc=1, device_id=(rep, (me + step) % peers), device_id_type=MESH
        )

    ends = ((mixed_far, mixed_ref), (images_far, images_ref), (proj_far, proj_ref), (captions_far, captions_ref))
    fetched = [pltpu.make_async_copy(*end, loads.at[number]) for number, end in enumerate(ends)]
    for fetch in fetched:
        fetch.start()

    def at(p):
        return pl.ds(pl.multiple_of(p * full, 8), full)

    def mover(src, dst, sends, recvs, flat):
        def move(p, home):
            return pltpu.make_async_remote_copy(
                src_ref=src.at[at(p) if flat else p],
                dst_ref=dst.at[at(home) if flat else home],
                send_sem=sends.at[p],
                recv_sem=recvs.at[home],
                device_id=(rep, p),
                device_id_type=MESH,
            )

        return move

    def keeper(src, dst, number, flat):
        here = at(me) if flat else me
        return pltpu.make_async_copy(src.at[here], dst.at[here], own_sem.at[number])

    moves = (
        (rows_out, rows_in, rs, rr, True),
        (picks_ref, picks_in, ps, pr, False),
        (chosen, got, bs, br, True),
        (rest_out, rest_in, es, er, False),
        (tail_out, tail_in, ts, tr, False),
    )
    rows_to, picks_to, back_to, rest_to, tail_to = [mover(*m) for m in moves]
    own_rows, own_picks, own_back, own_rest, own_tail = [
        keeper(m[0], m[1], number, m[4]) for number, m in enumerate(moves)
    ]
    keep = pltpu.make_async_copy(emb, emb_ref, own_sem.at[len(moves)])

    def farthest(place):
        found = z
        for zz in range(nz):
            order = sorted(
                range(nz), key=lambda other: (-abs(other - zz), (other < nz // 2) == (zz < nz // 2))
            )
            for turn in range(nz):
                found = jnp.where(jnp.logical_and(z == zz, place == turn), order[turn], found)
        return found

    def each(zz, local, remote):
        for part in range(4):
            p = zz * 4 + part

            @pl.when(p == me)
            def _():
                local()

            @pl.when(p != me)
            def _():
                remote(p)

    def each_plane(body):
        def step(turn, _):
            body(farthest(turn))
            return 0

        lax.fori_loop(0, nz, step, 0)

    pl.semaphore_wait(barrier, peers - 1)
    own_picks.start()
    for step in range(1, peers):
        picks_to((me + step) % peers, me).start()

    for fetch in fetched[:3]:
        fetch.wait()

    def embed(start, size):
        here = pl.ds(start, size)
        pick = lax.broadcasted_iota(jnp.int32, (size, tokens), 0) == slot_ref[...] - start
        onehot[here, :] = jnp.where(pick, 1.0, 0.0).astype(BF16)
        mine = onehot[here, :]
        left = jnp.dot(mine, mixed_ref[...], preferred_element_type=F32).astype(BF16)
        hidden = jnp.dot(mine, images_ref[...], preferred_element_type=F32) + dot_nt(left, proj_ref[...])
        inv_scale = lax.rsqrt(jnp.mean(hidden * hidden, axis=-1, keepdims=True) + 1e-06)
        return hidden * inv_scale

    def project(zz):
        start = pl.multiple_of(zz * block, block)
        rows_out[pl.ds(start, block), :] = embed(start, block).astype(BF16)
        each(zz, own_rows.start, lambda p: rows_to(p, me).start())

    each_plane(project)
    rest = embed(base, count)
    rows_out[base:base + count, :] = rest.astype(BF16)
    wide[...] = jnp.zeros_like(wide)
    tiles = width // 128
    for e in range(extra):
        for t in range(tiles):
            u = e * tiles + t
            wide[:, u % 8, u // 8 * 128:u // 8 * 128 + 128] = rest[
                e * peers:(e + 1) * peers, t * 128:(t + 1) * 128
            ]
    rest_out[...] = wide[...].astype(BF16)
    each_plane(lambda zz: each(zz, own_rest.start, lambda p: rest_to(p, me).start()))
    emb[...] = lax.dot_general(
        onehot[...], rows_out[...], (((0,), (0,)), ((), ())), preferred_element_type=F32
    ).astype(BF16)
    keep.start()

    def chosen_of(every, picks, k):
        pick = picks[:, k:k + 1]
        best = jnp.zeros((every.shape[0], CAPT), F32)
        for b in range(CBLK):
            best = jnp.where(pick == float(b), every[:, b * CAPT:(b + 1) * CAPT], best)
        return best

    def score(zz):
        here = pl.ds(pl.multiple_of(zz * block, block), block)

        def landed(p):
            picks_to(p, p).wait_recv()
            rows_to(p, p).wait_recv()

        def kept():
            own_picks.wait()
            own_rows.wait()

        each(zz, kept, landed)
        for part in range(4):
            p = zz * 4 + part
            turned = picks_in[p].astype(F32).T
            columns[part * full:(part + 1) * full] = turned[:full, :]
            for e in range(extra):
                rest_columns[pl.ds(e * peers + p, 1), :] = turned[full + e:full + e + 1, :]
        every = dot_nt(rows_in[here, :], captions_ref[...])
        for k in range(pick_count):
            chosen[here, k * CAPT:(k + 1) * CAPT] = chosen_of(every, columns, k).astype(BF16)
        each(zz, own_back.start, lambda p: back_to(p, me).start())

    fetched[3].wait()
    each_plane(score)
    each_plane(lambda zz: each(zz, own_rest.wait, lambda p: rest_to(p, p).wait_recv()))
    wide[...] = rest_in[...].astype(F32)
    for e in range(extra):
        for t in range(tiles):
            u = e * tiles + t
            part = wide[:, u % 8, u // 8 * 128:u // 8 * 128 + 128]
            rows_in[base + e * peers:base + (e + 1) * peers, t * 128:(t + 1) * 128] = part.astype(BF16)
    every = dot_nt(rows_in[base:base + count, :], captions_ref[...])
    tall[...] = jnp.zeros_like(tall)
    for k in range(pick_count):
        best = chosen_of(every, rest_columns, k)
        for e in range(extra):
            tall[:, e * pick_count + k, :] = best[e * peers:(e + 1) * peers]
    tail_out[...] = tall[...].astype(BF16)
    each_plane(lambda zz: each(zz, own_tail.start, lambda p: tail_to(p, me).start()))
    total[...] = jnp.zeros_like(total)

    def give(here):
        total[...] += lax.dot_general(
            onehot[here, :], got[here, :], (((0,), (0,)), ((), ())), preferred_element_type=F32
        )

    def take(zz):
        each(zz, own_back.wait, lambda p: back_to(p, p).wait_recv())
        give(pl.ds(pl.multiple_of(zz * block, block), block))

    each_plane(take)
    each_plane(lambda zz: each(zz, own_tail.wait, lambda p: tail_to(p, p).wait_recv()))
    tall[...] = tail_in[...].astype(F32)
    for k in range(pick_count):
        for e in range(extra):
            got[base + e * peers:base + (e + 1) * peers, k * CAPT:(k + 1) * CAPT] = tall[
                :, e * pick_count + k, :
            ].astype(BF16)
    give(pl.ds(base, count))
    for k in range(pick_count):
        out_ref[:, k, :] = total[:, k * CAPT:(k + 1) * CAPT].astype(BF16)
    keep.wait()

    def sent(p):
        for move in (rows_to, picks_to, back_to, rest_to, tail_to):
            move(p, me).wait_send()

    each_plane(lambda zz: each(zz, lambda: None, sent))


def back_call(mixed, w_proj, images, slot_row, picks, captions, pick_count):
    tokens, width = images.shape
    peers = picks.shape[0]
    full_rows, extra = split_of(tokens, peers)
    slots = peers * (full_rows + extra)
    rest_shape = (peers, 8, -(-extra * (width // 128) // 8) * 128)
    tail_shape = (peers, -(-extra * pick_count // 8) * 8, CAPT)
    anywhere = pl.BlockSpec(memory_space=pl.ANY)
    full = pl.BlockSpec(memory_space=VMEM)
    dma = pltpu.SemaphoreType.DMA
    return pl.pallas_call(
        back_kernel,
        in_specs=[anywhere] * 3 + [full] * 2 + [anywhere],
        out_specs=(anywhere, full),
        out_shape=(
            jax.ShapeDtypeStruct((tokens, width), BF16),
            jax.ShapeDtypeStruct((tokens, pick_count, CAPT), BF16),
        ),
        scratch_shapes=[
            VMEM(mixed.shape, BF16),
            VMEM(w_proj.shape, BF16),
            VMEM(images.shape, BF16),
            VMEM(captions.shape, BF16),
            dma((4,)),
            VMEM((slots, tokens), BF16),
            VMEM((slots, width), BF16),
            VMEM((slots, width), BF16),
            VMEM(picks.shape, BF16),
            VMEM((slots, pick_count * CAPT), BF16),
            VMEM((slots, pick_count * CAPT), BF16),
            VMEM((4 * full_rows, picks.shape[1]), F32),
            VMEM((peers * extra, picks.shape[1]), F32),
            VMEM((tokens, width), BF16),
            VMEM((tokens, pick_count * CAPT), F32),
            VMEM(rest_shape, F32),
            VMEM(rest_shape, BF16),
            VMEM(rest_shape, BF16),
            VMEM(tail_shape, F32),
            VMEM(tail_shape, BF16),
            VMEM(tail_shape, BF16),
        ]
        + [dma((peers,))] * 10
        + [dma((6,))],
        compiler_params=pltpu.CompilerParams(
            collective_id=1, has_side_effects=True, vmem_limit_bytes=BACK_LIMIT
        ),
        name="back",
    )(mixed, w_proj, images, slot_row, picks, captions)


def return_kernel(slot_ref, rows_ref, out_ref, *packed):
    if packed:
        (flat,) = packed
        flat[...] = jnp.zeros_like(flat)
        stride = flat.shape[0] // rows_ref.shape[0]
        for p in range(rows_ref.shape[0]):
            flat[p * stride:p * stride + rows_ref.shape[1], :] = rows_ref[p]
        rows = flat[...]
    else:
        rows = rows_ref[...]
    tokens, slots = out_ref.shape[0], rows.shape[0]
    pick = lax.broadcasted_iota(jnp.int32, (tokens, slots), 1) == slot_ref[...]
    onehot = jnp.where(pick, 1.0, 0.0).astype(BF16)
    got = jnp.dot(onehot, rows, preferred_element_type=F32).astype(BF16)
    for k in range(out_ref.shape[1]):
        out_ref[:, k, :] = got[:, k * CAPT:(k + 1) * CAPT]


def return_call(slot_col, rows, pick_count):
    full = pl.BlockSpec(memory_space=VMEM)
    return pl.pallas_call(
        return_kernel,
        in_specs=[full] * 2,
        out_specs=full,
        out_shape=jax.ShapeDtypeStruct((slot_col.shape[0], pick_count, CAPT), BF16),
        scratch_shapes=[pltpu.VMEM((rows.shape[0] * stride_of(rows.shape[1]), rows.shape[2]), BF16)]
        if rows.ndim == 3
        else [],
        compiler_params=pltpu.CompilerParams(vmem_limit_bytes=VLIMIT),
        name="give_back",
    )(slot_col, rows)


def local(
    images,
    norm_gain,
    qkv_values,
    qkv_exponents,
    proj_values,
    proj_exponents,
    captions,
    owners,
    candidates,
):
    token_count, width = images.shape
    peer_count = lax.axis_size("idx")
    me = lax.axis_index("idx")
    capacity = capacity_of(token_count, peer_count)

    def own_exponents(exponents, cols):
        return lax.dynamic_slice_in_dim(exponents, me * cols, cols, axis=1)

    qkv_cols, proj_cols = qkv_values.shape[1], proj_values.shape[1]
    qkv_own = dequant_rows(qkv_values, own_exponents(qkv_exponents, qkv_cols))
    proj_own = dequant_rows(proj_values, own_exponents(proj_exponents, proj_cols))
    joined = fits(images, qkv_own, proj_own, peer_count, lax.axis_size("rep"))

    owner_ids = owners[:, 0]
    onehot = (owner_ids[:, None] == jnp.arange(peer_count, dtype=jnp.int32)[None, :]).astype(
        jnp.int32
    )
    slot_rank = jnp.sum((jnp.cumsum(onehot, axis=0) - onehot) * onehot, axis=1)
    stride = stride_of(capacity) if joined else capacity
    slot_index = owner_ids * stride + slot_rank
    slots = peer_count * stride
    pick_count = candidates.shape[1]
    dispatch = (jnp.arange(slots, dtype=jnp.int32)[:, None] == slot_index[None, :]).astype(BF16)
    send_picks = jnp.dot(dispatch, candidates.astype(BF16), preferred_element_type=F32).astype(BF16)
    gain = norm_gain[None, :]
    if joined:
        turned = send_picks.reshape(peer_count, stride, pick_count).transpose(0, 2, 1)
        turned = jnp.pad(turned, ((0, 0), (0, 8 - pick_count), (0, 128 - stride)))
        whole, _ = split_of(token_count, peer_count)
        place = jnp.where(
            slot_rank < whole,
            owner_ids * whole + slot_rank,
            peer_count * slot_rank + owner_ids,
        )
        mixed, w_proj = front_call(images, gain, qkv_own, proj_own, peer_count)
        return back_call(
            mixed, w_proj.reshape(width, width), images, place[None, :], turned, captions, pick_count
        )
    w_qkv, w_proj = (lax.all_gather(own, "idx", axis=0, tiled=True) for own in (qkv_own, proj_own))
    qkv = qkv_call(images, gain, w_qkv)
    embedding, send_rows = attend_call(qkv, w_proj, images, slot_index[None, :], (slots,))

    def swap(blocks):
        shaped = blocks.reshape(peer_count, capacity, blocks.shape[1])
        moved = lax.all_to_all(shaped, "idx", split_axis=0, concat_axis=0, tiled=True)
        return moved.reshape(blocks.shape)

    returned = swap(score_call(swap(send_rows), swap(send_picks), captions))
    return (embedding, return_call(slot_index[:, None], returned, pick_count))


def solution(mesh):
    placed = (
        P(("rep", "idx"), None),
        P(),
        P(None, "idx"),
        P(),
        P(None, "idx"),
        P(),
        P(("rep", "idx"), None),
        P(("rep", "idx"), None),
        P(("rep", "idx"), None),
    )
    return jax.shard_map(
        local,
        mesh=mesh,
        in_specs=placed,
        out_specs=(P(("rep", "idx"), None), P(("rep", "idx"), None, None)),
        check_vma=False,
    )
```

```python
import math
import jax
import jax.numpy as jnp
from jax import lax
from jax.experimental import pallas as pl
from jax.experimental.pallas import tpu as pltpu
from jax.sharding import PartitionSpec as P

HEADS = 16
PATCHES = 257
CBLK = 8
CAPT = 128
F32 = jnp.float32
BF16 = jnp.bfloat16
VMEM = pltpu.VMEM
VLIMIT = 60 * 1024 * 1024


def dequant_rows(stored, exponents):
    row_count, col_count = stored.shape
    block_count = exponents.shape[0]
    turned = stored.T.astype(F32).reshape(col_count, block_count, row_count // block_count)
    scaled = turned * jnp.exp2(exponents.astype(F32)).T[:, :, None]
    return scaled.reshape(col_count, row_count).astype(BF16)


def layer_norm(token_rows, norm_gain):
    values = token_rows.astype(F32)
    centered = values - jnp.mean(values, axis=-1, keepdims=True)
    inv_scale = lax.rsqrt(jnp.mean(centered * centered, axis=-1, keepdims=True) + 1e-06)
    return (centered * inv_scale * norm_gain).astype(BF16)


def dot_nt(left, right):
    return lax.dot_general(left, right, (((1,), (1,)), ((), ())), preferred_element_type=F32)


MESH = pl.DeviceIdType.MESH

FRONT_LIMIT = 66_800_000
BACK_LIMIT = 64_600_000


def spans_of(rows):
    third = rows // 24 * 8
    return (0, rows - 2 * third), (rows - 2 * third, third), (rows - third, third)


def powers_of_two(exponents):
    found = jnp.ones(exponents.shape, F32)
    for power in (-2, -1, 1, 2):
        found = jnp.where(exponents == power, 2.0 ** power, found)
    return found


def scale_own(stored_ref, exponents_ref, own_ref, me):
    cols, block_count = stored_ref.shape[0], exponents_ref.shape[0]
    block = stored_ref.shape[1] // block_count
    span = -(-(cols + 127) // 128) * 128
    first = jnp.minimum(me * cols // 128, (exponents_ref.shape[1] - span) // 128) * 128
    near = exponents_ref[:, pl.ds(pl.multiple_of(first, 128), span)]
    ahead = lax.broadcasted_iota(jnp.int32, (cols, span), 1) - lax.broadcasted_iota(
        jnp.int32, (cols, span), 0
    )
    pick = jnp.where(ahead == me * cols - first, 1.0, 0.0).astype(BF16)
    turned = dot_nt(pick, powers_of_two(near).astype(BF16))
    for b in range(block_count):
        here = slice(b * block, (b + 1) * block)
        own_ref[:, here] = (stored_ref[:, here].astype(F32) * turned[:, b:b + 1]).astype(BF16)


def place_tokens(owner_ref, candidates_ref, place_ref, picks_ref):
    peers, tokens = picks_ref.shape[0], owner_ref.shape[1]
    pick_count = candidates_ref.shape[0]
    whole, _ = split_of(tokens, peers)
    owner = owner_ref[...]
    hot = jnp.where(lax.broadcasted_iota(jnp.int32, (peers, tokens), 0) == owner, 1.0, 0.0)
    earlier = lax.broadcasted_iota(jnp.int32, (tokens, tokens), 0) < lax.broadcasted_iota(
        jnp.int32, (tokens, tokens), 1
    )
    counts = jnp.dot(
        hot.astype(BF16), jnp.where(earlier, 1.0, 0.0).astype(BF16), preferred_element_type=F32
    )
    rank = jnp.sum(counts * hot, axis=0, keepdims=True)
    name = owner.astype(F32)
    place_ref[...] = jnp.where(rank < whole, name * whole + rank, rank * peers + name)
    named = candidates_ref[...].astype(F32)
    unused = jnp.zeros((picks_ref.shape[1] - pick_count, tokens), F32)
    named = jnp.concatenate([named, unused], axis=0).astype(BF16)
    lanes = picks_ref.shape[2]
    slot = lax.broadcasted_iota(jnp.int32, (lanes, tokens), 0).astype(F32)

    def fill(p, _):
        wanted = jnp.where(owner == p, rank, -1.0)
        pick = jnp.where(slot == wanted, 1.0, 0.0).astype(BF16)
        picks_ref[p] = dot_nt(named, pick).astype(BF16)
        return 0

    lax.fori_loop(0, peers, fill, 0)


def front_kernel(
    images_far, q_stored_far, p_stored_far, q_exponents_far, p_exponents_far, owner_far,
    candidates_far, gain_far, mixed_ref, p_out, place_ref, picks_ref,
    images_ref, q_stored, p_stored, q_exponents, p_exponents, owner_ref, candidates_ref, gain_ref,
    loads, q_own, p_own,
    q_all, normed, qkv, mixed, rz, ry, rx, rc, sz, sy, sx, sc, held,
):
    peers = q_all.shape[0]
    nz = peers // 4
    group, units, head_dim, patches = qkv.shape
    lanes = normed.shape[0] // group
    share = units // peers
    me = lax.axis_index("idx")
    x = lax.axis_index("rep")
    z, y, c = me // 4, (me // 2) % 2, me % 2
    own, out = (q_own, p_own), (q_all, p_out)
    ends = (
        (images_far, images_ref),
        (q_stored_far, q_stored),
        (p_stored_far, p_stored),
        (q_exponents_far, q_exponents),
        (p_exponents_far, p_exponents),
        (owner_far, owner_ref),
        (candidates_far, candidates_ref),
        (gain_far, gain_ref.at[0]),
    )
    fetched = [pltpu.make_async_copy(*end, loads.at[number]) for number, end in enumerate(ends)]
    for number in (3, 4, 1, 2, 0, 5, 6, 7):
        fetched[number].start()

    def at(zz, yy, cc):
        return (zz * 2 + yy) * 2 + cc

    to_y, to_c, to_x = (x, at(z, 1 - y, c)), (x, at(z, y, 1 - c)), (1 - x, me)
    to_up, to_down = (x, me + 4), (x, me - 4)
    barrier = pltpu.get_barrier_semaphore()

    def greet(target):
        pl.semaphore_signal(barrier, inc=1, device_id=target, device_id_type=MESH)

    for target in (to_y, to_c, to_x):
        greet(target)

    @pl.when(z + 1 < nz)
    def _():
        greet(to_up)

    @pl.when(z > 0)
    def _():
        greet(to_down)

    for number in (1, 2, 3, 4):
        fetched[number].wait()
    scale_own(q_stored, q_exponents, q_own, me)
    scale_own(p_stored, p_exponents, p_own, me)
    greeted = 3 + jnp.where(z + 1 < nz, 1, 0) + jnp.where(z > 0, 1, 0)
    pl.semaphore_wait(barrier, greeted)

    def rows(a, k):
        spans = spans_of(own[a].shape[0])
        if k == 0:
            return pl.ds(*spans[0])
        if k == 3:
            return pl.ds(0, own[a].shape[0])
        side = x if k == 1 else 1 - x
        return pl.ds(pl.multiple_of(spans[1][0] + spans[1][1] * side, 8), spans[1][1])

    def copy(a, shard, k, mine, send, recv, target):
        span = rows(a, k)
        return pltpu.make_async_remote_copy(
            src_ref=own[a].at[span] if mine else out[a].at[shard, span],
            dst_ref=out[a].at[shard, span],
            send_sem=send,
            recv_sem=recv,
            device_id=target,
            device_id_type=MESH,
        )

    def pos(zz, yy):
        return zz * 2 + yy

    def up(a, zz, k, mine=False):
        return copy(a, at(zz, y, c), k, mine, sz.at[0, a, zz, k], rz.at[a, zz, k], to_up)

    def down(a, zz, k, mine=False):
        return copy(a, at(zz, y, c), k, mine, sz.at[1, a, zz, k], rz.at[a, zz, k], to_down)

    def across(a, zz, k, yy, mine=False):
        return copy(a, at(zz, yy, c), k, mine, sy.at[a, zz, k], ry.at[a, zz, k], to_y)

    def plane(a, zz, yy, k):
        return copy(a, at(zz, yy, c), k, False, sx.at[a, pos(zz, yy)], rx.at[a, pos(zz, yy)], to_x)

    def core(a, zz, yy, cc, k, mine=False):
        slot = 0 if k == 3 else k
        return copy(
            a, at(zz, yy, cc), k, mine, sc.at[a, pos(zz, yy), slot], rc.at[a, pos(zz, yy), slot], to_c
        )

    def each(distance, body):
        if distance == 0:
            body(z, 0)
            return

        @pl.when(z - distance >= 0)
        def _():
            body(z - distance, -1)

        @pl.when(z + distance < nz)
        def _():
            body(z + distance, 1)

    def start_own(a):
        for k in (1, 0):

            @pl.when(z + 1 < nz)
            def _():
                up(a, z, k, True).start()

            @pl.when(z > 0)
            def _():
                down(a, z, k, True).start()

            across(a, z, k, y, True).start()
        core(a, z, y, c, 3, True).start()
        pltpu.make_async_copy(own[a], out[a].at[me], held.at[a]).start()

    def chain_event(a, step, kinds):
        def body(zz, side):
            for k in kinds:
                up(a, zz, k).wait_recv()
                if side < 0:

                    @pl.when(z + 1 < nz)
                    def _():
                        up(a, zz, k).start()
                else:

                    @pl.when(z > 0)
                    def _():
                        down(a, zz, k).start()

                across(a, zz, k, y).start()
                if k == 1:
                    plane(a, zz, y, 1).start()
                core(a, zz, y, c, k).start()

        each(step, body)

    def across_event(a, distance, kinds):
        def body(zz, side):
            for k in kinds:
                across(a, zz, k, 1 - y).wait_recv()
                if k == 1:
                    plane(a, zz, 1 - y, 1).start()
                core(a, zz, 1 - y, c, k).start()

        each(distance, body)

    def plane_event(a, distance):
        def body(zz, side):
            if side != 0:
                plane(a, zz, y, 2).wait_recv()
                core(a, zz, y, c, 2).start()
            plane(a, zz, 1 - y, 2).wait_recv()
            core(a, zz, 1 - y, c, 2).start()

        each(distance, body)

    def run(listed):
        for event in listed:
            a = int(event[-1] if event[0] == "o" else event[1])
            if event[0] == "o":
                start_own(a)
                continue
            distance, kinds = int(event[2]), tuple(int(k) for k in event[3:])
            if event[0] == "c":
                chain_event(a, distance, kinds)
            elif event[0] == "x":
                across_event(a, distance, kinds)
            else:
                plane_event(a, distance)

    def nearest(place):
        found = z
        for zz in range(nz):
            order = sorted(range(nz), key=lambda other: (abs(other - zz), other))
            for turn in range(nz):
                hit = jnp.logical_and(z == zz, place == turn)
                found = jnp.where(hit, order[turn], found)
        return found

    def settle(a, zz):
        @pl.when(zz == z)
        def _():
            pltpu.make_async_copy(own[a], out[a].at[me], held.at[a]).wait()
            core(a, z, y, 1 - c, 3).wait_recv()
            for k in (1, 0, 2):
                core(a, z, 1 - y, 1 - c, k).wait_recv()

        @pl.when(zz != z)
        def _():
            for yy in (y, 1 - y):
                for k in (1, 0, 2):
                    core(a, zz, yy, 1 - c, k).wait_recv()

    def qkv_step(turn, _):
        zz = nearest(turn // 4)
        for number, listed in enumerate(QKV_EVENTS):
            if listed:

                @pl.when(turn == number)
                def _():
                    run(listed)

        @pl.when(turn % 4 == 0)
        def _():
            settle(0, zz)

        shard = zz * 4 + turn % 4
        every = dot_nt(q_all[shard], normed[...])
        for g in range(group):
            found = every[:, g * lanes:g * lanes + patches].reshape(share, head_dim, patches)
            qkv[g, pl.ds(shard * share, share)] = found.astype(BF16)
        return 0

    scale = head_dim ** (-0.5)
    bunch = 4
    rounds = HEADS // bunch

    def head_step(turn, _):
        for number, listed in enumerate(HEAD_EVENTS):
            if listed:

                @pl.when(turn == number)
                def _():
                    run(listed)

        g = turn // rounds
        for b in range(bunch):
            h = (turn % rounds) * bunch + b
            queries, keys, vals = qkv[g, h], qkv[g, HEADS + h], qkv[g, 2 * HEADS + h]
            logits = lax.dot_general(
                keys, queries, (((0,), (0,)), ((), ())), preferred_element_type=F32
            )
            logits = logits * scale
            weights = jnp.exp(logits - jnp.max(logits, axis=0, keepdims=True))
            probs = weights * (1.0 / jnp.sum(weights, axis=0, keepdims=True))
            found = jnp.dot(vals, probs.astype(BF16), preferred_element_type=F32)
            mixed[pl.ds(pl.multiple_of(h * head_dim, 8), head_dim), :] = found
        for image in range(group):

            @pl.when(turn == image * rounds + rounds - 1)
            def _():
                mixed_ref[image * patches:(image + 1) * patches] = mixed[...].T.astype(BF16)

        return 0

    run(LEAD_EVENTS)
    for number in (0, 5, 6, 7):
        fetched[number].wait()
    normed[...] = jnp.zeros_like(normed)
    for g in range(group):
        normed[g * lanes:g * lanes + patches] = layer_norm(
            images_ref[g * patches:(g + 1) * patches], gain_ref[...]
        )
    place_tokens(owner_ref, candidates_ref, place_ref, picks_ref)
    lax.fori_loop(0, len(QKV_EVENTS), qkv_step, 0)
    lax.fori_loop(0, group * rounds, head_step, 0)
    run(LAST_EVENTS)
    for zz in range(nz):
        settle(1, zz)

    for a in range(2):
        for distance in range(nz):

            def finish(zz, side):
                first = side == 0
                for k in (1, 0):
                    if side <= 0:

                        @pl.when(z + 1 < nz)
                        def _():
                            up(a, zz, k, first).wait_send()

                    if side >= 0:

                        @pl.when(z > 0)
                        def _():
                            down(a, zz, k, first).wait_send()

                    across(a, zz, k, y, first).wait_send()
                for yy, mine in ((y, first), (1 - y, False)):
                    if mine:
                        core(a, zz, yy, c, 3, True).wait_send()
                        continue
                    plane(a, zz, yy, 1).wait_send()
                    for k in (1, 0, 2):
                        core(a, zz, yy, c, k).wait_send()

            each(distance, finish)


LEAD_EVENTS = ("own0", "x001", "c011",)
LEAD_EVENTS = ("own0", "x001", "c011", "c010", "x000", "x011", "p00", "c021",)
QKV_EVENTS = (
    (),
    ("c020", "p01",),
    ("x010",),
    (),
    ("x021", "c031", "c030",),
    (),
    ("own1",),
    ("x031",),
    ("x020", "p02", "c111", "x030", "p03",),
    ("c110",),
    (),
    ("x101",),
    (),
    ("c121",),
    (),
    (),
)
HEAD_EVENTS = (
    ("x111", "c120",),
    ("c131",),
    ("x110",),
    ("x121", "c130",),
    ("p11", "p10", "x131", "x100",),
    ("x120",),
    ("x130", "p12",),
    ("p13",),
)
LAST_EVENTS = ()


def fits(images, q_cols, p_cols, q_blocks, peers, reps):
    tokens, width = images.shape
    rows_whole = q_cols % 88 == 0 and p_cols % 88 == 0 and width == q_blocks * 128
    layout = peers == len(QKV_EVENTS) and reps == 2
    return layout and rows_whole and width == peers * p_cols and tokens % PATCHES == 0


def front_call(images, gain, q_stored, p_stored, q_exponents, p_exponents, owner_row, candidates, peers):
    tokens, width = images.shape
    group = tokens // PATCHES
    head_dim = width // HEADS
    lanes = -(-PATCHES // 128) * 128
    full = pl.BlockSpec(memory_space=VMEM)
    nz = peers // 4
    dma = pltpu.SemaphoreType.DMA
    return pl.pallas_call(
        front_kernel,
        in_specs=[pl.BlockSpec(memory_space=pltpu.HBM)] * 8,
        out_specs=(full, pl.BlockSpec(memory_space=pl.ANY), full, full),
        out_shape=(
            jax.ShapeDtypeStruct((tokens, width), BF16),
            jax.ShapeDtypeStruct((peers,) + p_stored.shape, BF16),
            jax.ShapeDtypeStruct((1, tokens), F32),
            jax.ShapeDtypeStruct((peers, 8, 128), BF16),
        ),
        scratch_shapes=[
            VMEM(images.shape, BF16),
            VMEM(q_stored.shape, BF16),
            VMEM(p_stored.shape, BF16),
            VMEM(q_exponents.shape, jnp.int32),
            VMEM(p_exponents.shape, jnp.int32),
            VMEM(owner_row.shape, jnp.int32),
            VMEM(candidates.shape, jnp.int32),
            VMEM((1, width), F32),
            dma((8,)),
            VMEM(q_stored.shape, BF16),
            VMEM(p_stored.shape, BF16),
            pltpu.VMEM((peers,) + q_stored.shape, BF16),
            pltpu.VMEM((group * lanes, width), BF16),
            pltpu.VMEM((group, 3 * HEADS, head_dim, PATCHES), BF16),
            pltpu.VMEM((width, PATCHES), F32),
            dma((2, nz, 2)),
            dma((2, nz, 2)),
            dma((2, 2 * nz)),
            dma((2, 2 * nz, 3)),
            dma((2, 2, nz, 2)),
            dma((2, nz, 2)),
            dma((2, 2 * nz)),
            dma((2, 2 * nz, 3)),
            dma((2,)),
        ],
        compiler_params=pltpu.CompilerParams(
            collective_id=0, has_side_effects=True, vmem_limit_bytes=FRONT_LIMIT
        ),
        name="front",
    )(images, q_stored, p_stored, q_exponents, p_exponents, owner_row, candidates, gain)


def qkv_kernel(images_ref, gain_ref, w_ref, out_ref, normed):
    group, unit, head_dim = out_ref.shape[0], out_ref.shape[1], out_ref.shape[2]

    @pl.when(pl.program_id(0) == 0)
    def _():
        normed[...] = layer_norm(images_ref[...], gain_ref[...])

    patches = out_ref.shape[3]
    every = dot_nt(w_ref[...], normed[...])
    for g in range(group):
        rows = every[:, g * patches:(g + 1) * patches]
        out_ref[g] = rows.reshape(unit, head_dim, patches).astype(BF16)


def qkv_call(images, gain, w_rows):
    tokens, width = images.shape
    patches = PATCHES
    group = tokens // patches
    head_dim = width // HEADS
    units = w_rows.shape[0] // head_dim
    step = 4
    return pl.pallas_call(
        qkv_kernel,
        grid=(units // step,),
        in_specs=[
            pl.BlockSpec((tokens, width), lambda i: (0, 0)),
            pl.BlockSpec((1, width), lambda i: (0, 0)),
            pl.BlockSpec((step * head_dim, width), lambda i: (i, 0)),
        ],
        out_specs=pl.BlockSpec((group, step, head_dim, patches), lambda i: (0, i, 0, 0)),
        out_shape=jax.ShapeDtypeStruct((group, units, head_dim, patches), BF16),
        scratch_shapes=[pltpu.VMEM((tokens, width), BF16)],
        compiler_params=pltpu.CompilerParams(vmem_limit_bytes=VLIMIT),
        name="qkv",
    )(images, gain, w_rows)


def attend_kernel(qkv_ref, proj_ref, images_ref, slot_ref, emb_ref, send_ref, mixed):
    group, units, head_dim, patches = qkv_ref.shape
    width = HEADS * head_dim
    scale = head_dim ** (-0.5)
    for g in range(group):

        @pl.loop(0, HEADS, unroll=4)
        def _(h):
            queries, keys, vals = qkv_ref[g, h], qkv_ref[g, HEADS + h], qkv_ref[g, 2 * HEADS + h]
            logits = lax.dot_general(
                keys, queries, (((0,), (0,)), ((), ())), preferred_element_type=F32
            )
            logits = logits * scale
            weights = jnp.exp(logits - jnp.max(logits, axis=0, keepdims=True))
            probs = weights * (1.0 / jnp.sum(weights, axis=0, keepdims=True))
            out = jnp.dot(vals, probs.astype(BF16), preferred_element_type=F32)
            mixed[pl.ds(pl.multiple_of(h * head_dim, 8), head_dim), :] = out

        left = mixed[...].T.astype(BF16)
        hidden = images_ref[g * patches:(g + 1) * patches, :].astype(F32) + dot_nt(left, proj_ref[...])
        inv_scale = lax.rsqrt(jnp.mean(hidden * hidden, axis=-1, keepdims=True) + 1e-06)
        emb_ref[g * patches:(g + 1) * patches, :] = (hidden * inv_scale).astype(BF16)
    slots = math.prod(send_ref.shape[:-1])
    tokens = group * patches
    pick = lax.broadcasted_iota(jnp.int32, (slots, tokens), 0) == slot_ref[...]
    onehot = jnp.where(pick, 1.0, 0.0).astype(BF16)
    sent = jnp.dot(onehot, emb_ref[...], preferred_element_type=F32).astype(BF16)
    if len(send_ref.shape) == 2:
        send_ref[...] = sent
        return
    peers, capacity = send_ref.shape[0], send_ref.shape[1]
    for p in range(peers):
        send_ref[p] = sent[p * capacity:(p + 1) * capacity]


def attend_call(qkv, w_proj, images, slot_row, slot_shape):
    tokens, width = images.shape
    patches = qkv.shape[3]
    group = tokens // patches
    full = pl.BlockSpec(memory_space=VMEM)
    return pl.pallas_call(
        attend_kernel,
        in_specs=[full] * 4,
        out_specs=(full, full),
        out_shape=(
            jax.ShapeDtypeStruct((group * patches, width), BF16),
            jax.ShapeDtypeStruct(slot_shape + (width,), BF16),
        ),
        scratch_shapes=[pltpu.VMEM((width, patches), F32)],
        compiler_params=pltpu.CompilerParams(vmem_limit_bytes=VLIMIT),
        name="attend",
    )(qkv, w_proj, images, slot_row)


def score_kernel(rows_ref, picks_ref, captions_ref, out_ref):
    every = dot_nt(rows_ref[...], captions_ref[...]).astype(BF16)
    for k in range(picks_ref.shape[1]):
        pick = picks_ref[:, k:k + 1].astype(F32)
        chosen = jnp.zeros((every.shape[0], CAPT), F32)
        for b in range(CBLK):
            block = every[:, b * CAPT:(b + 1) * CAPT].astype(F32)
            chosen = jnp.where(pick == float(b), block, chosen)
        out_ref[:, k * CAPT:(k + 1) * CAPT] = chosen.astype(BF16)


def score_call(rows, picks, captions):
    full = pl.BlockSpec(memory_space=VMEM)
    return pl.pallas_call(
        score_kernel,
        in_specs=[full] * 3,
        out_specs=full,
        out_shape=jax.ShapeDtypeStruct((rows.shape[0], picks.shape[1] * CAPT), BF16),
        compiler_params=pltpu.CompilerParams(vmem_limit_bytes=VLIMIT),
        name="score",
    )(rows, picks, captions)


def capacity_of(tokens, peers):
    return (tokens + peers - 1) // peers + 1


def split_of(tokens, peers):
    capacity = capacity_of(tokens, peers)
    return capacity // 8 * 8, capacity % 8


def stride_of(capacity):
    return -(-capacity // 8) * 8


def back_kernel(
    mixed_far, proj_far, images_far, slot_ref, picks_ref, captions_far, emb_ref, out_ref,
    mixed_ref, proj_ref, images_ref, captions_ref, loads,
    onehot, rows_out, rows_in, picks_in, chosen, got, columns, rest_columns, emb, total,
    wide, rest_out, rest_in, tall, tail_out, tail_in,
    rs, rr, ps, pr, bs, br, es, er, ts, tr, own_sem,
):
    peers = picks_ref.shape[0]
    tokens = slot_ref.shape[1]
    width = rows_out.shape[1]
    full, extra = split_of(tokens, peers)
    base, count = peers * full, peers * extra
    pick_count = out_ref.shape[1]
    nz, block = peers // 4, 4 * full
    me = lax.axis_index("idx")
    rep = lax.axis_index("rep")
    z = me // 4
    barrier = pltpu.get_barrier_semaphore()
    for step in range(1, peers):
        pl.semaphore_signal(
            barrier, inc=1, device_id=(rep, (me + step) % peers), device_id_type=MESH
        )

    ends = ((mixed_far, mixed_ref), (images_far, images_ref), (proj_far, proj_ref), (captions_far, captions_ref))
    fetched = [pltpu.make_async_copy(*end, loads.at[number]) for number, end in enumerate(ends)]
    for fetch in fetched:
        fetch.start()

    def at(p):
        return pl.ds(pl.multiple_of(p * full, 8), full)

    def mover(src, dst, sends, recvs, flat):
        def move(p, home):
            return pltpu.make_async_remote_copy(
                src_ref=src.at[at(p) if flat else p],
                dst_ref=dst.at[at(home) if flat else home],
                send_sem=sends.at[p],
                recv_sem=recvs.at[home],
                device_id=(rep, p),
                device_id_type=MESH,
            )

        return move

    def keeper(src, dst, number, flat):
        here = at(me) if flat else me
        return pltpu.make_async_copy(src.at[here], dst.at[here], own_sem.at[number])

    moves = (
        (rows_out, rows_in, rs, rr, True),
        (picks_ref, picks_in, ps, pr, False),
        (chosen, got, bs, br, True),
        (rest_out, rest_in, es, er, False),
        (tail_out, tail_in, ts, tr, False),
    )
    rows_to, picks_to, back_to, rest_to, tail_to = [mover(*m) for m in moves]
    own_rows, own_picks, own_back, own_rest, own_tail = [
        keeper(m[0], m[1], number, m[4]) for number, m in enumerate(moves)
    ]
    keep = pltpu.make_async_copy(emb, emb_ref, own_sem.at[len(moves)])

    def farthest(place):
        found = z
        for zz in range(nz):
            order = sorted(
                range(nz), key=lambda other: (-abs(other - zz), (other < nz // 2) == (zz < nz // 2))
            )
            for turn in range(nz):
                found = jnp.where(jnp.logical_and(z == zz, place == turn), order[turn], found)
        return found

    def each(zz, local, remote):
        for part in range(4):
            p = zz * 4 + part

            @pl.when(p == me)
            def _():
                local()

            @pl.when(p != me)
            def _():
                remote(p)

    def each_plane(body):
        def step(turn, _):
            body(farthest(turn))
            return 0

        lax.fori_loop(0, nz, step, 0)

    pl.semaphore_wait(barrier, peers - 1)
    own_picks.start()
    for step in range(1, peers):
        picks_to((me + step) % peers, me).start()

    for fetch in fetched[:3]:
        fetch.wait()

    def embed(start, size):
        here = pl.ds(start, size)
        pick = lax.broadcasted_iota(jnp.int32, (size, tokens), 0) == slot_ref[...].astype(jnp.int32) - start
        onehot[here, :] = jnp.where(pick, 1.0, 0.0).astype(BF16)
        mine = onehot[here, :]
        left = jnp.dot(mine, mixed_ref[...], preferred_element_type=F32).astype(BF16)
        hidden = jnp.dot(mine, images_ref[...], preferred_element_type=F32) + dot_nt(left, proj_ref[...])
        inv_scale = lax.rsqrt(jnp.mean(hidden * hidden, axis=-1, keepdims=True) + 1e-06)
        return hidden * inv_scale

    def project(zz):
        start = pl.multiple_of(zz * block, block)
        rows_out[pl.ds(start, block), :] = embed(start, block).astype(BF16)
        each(zz, own_rows.start, lambda p: rows_to(p, me).start())

    each_plane(project)
    rest = embed(base, count)
    rows_out[base:base + count, :] = rest.astype(BF16)
    wide[...] = jnp.zeros_like(wide)
    tiles = width // 128
    for e in range(extra):
        for t in range(tiles):
            u = e * tiles + t
            wide[:, u % 8, u // 8 * 128:u // 8 * 128 + 128] = rest[
                e * peers:(e + 1) * peers, t * 128:(t + 1) * 128
            ]
    rest_out[...] = wide[...].astype(BF16)
    each_plane(lambda zz: each(zz, own_rest.start, lambda p: rest_to(p, me).start()))
    emb[...] = lax.dot_general(
        onehot[...], rows_out[...], (((0,), (0,)), ((), ())), preferred_element_type=F32
    ).astype(BF16)
    keep.start()

    def chosen_of(every, picks, k):
        pick = picks[:, k:k + 1]
        best = jnp.zeros((every.shape[0], CAPT), F32)
        for b in range(CBLK):
            best = jnp.where(pick == float(b), every[:, b * CAPT:(b + 1) * CAPT], best)
        return best

    def score(zz):
        here = pl.ds(pl.multiple_of(zz * block, block), block)

        def landed(p):
            picks_to(p, p).wait_recv()
            rows_to(p, p).wait_recv()

        def kept():
            own_picks.wait()
            own_rows.wait()

        each(zz, kept, landed)
        for part in range(4):
            p = zz * 4 + part
            turned = picks_in[p].astype(F32).T
            columns[part * full:(part + 1) * full] = turned[:full, :]
            for e in range(extra):
                rest_columns[pl.ds(e * peers + p, 1), :] = turned[full + e:full + e + 1, :]
        every = dot_nt(rows_in[here, :], captions_ref[...])
        for k in range(pick_count):
            chosen[here, k * CAPT:(k + 1) * CAPT] = chosen_of(every, columns, k).astype(BF16)
        each(zz, own_back.start, lambda p: back_to(p, me).start())

    fetched[3].wait()
    each_plane(score)
    each_plane(lambda zz: each(zz, own_rest.wait, lambda p: rest_to(p, p).wait_recv()))
    wide[...] = rest_in[...].astype(F32)
    for e in range(extra):
        for t in range(tiles):
            u = e * tiles + t
            part = wide[:, u % 8, u // 8 * 128:u // 8 * 128 + 128]
            rows_in[base + e * peers:base + (e + 1) * peers, t * 128:(t + 1) * 128] = part.astype(BF16)
    every = dot_nt(rows_in[base:base + count, :], captions_ref[...])
    tall[...] = jnp.zeros_like(tall)
    for k in range(pick_count):
        best = chosen_of(every, rest_columns, k)
        for e in range(extra):
            tall[:, e * pick_count + k, :] = best[e * peers:(e + 1) * peers]
    tail_out[...] = tall[...].astype(BF16)
    each_plane(lambda zz: each(zz, own_tail.start, lambda p: tail_to(p, me).start()))
    total[...] = jnp.zeros_like(total)

    def give(here):
        total[...] += lax.dot_general(
            onehot[here, :], got[here, :], (((0,), (0,)), ((), ())), preferred_element_type=F32
        )

    def take(zz):
        each(zz, own_back.wait, lambda p: back_to(p, p).wait_recv())
        give(pl.ds(pl.multiple_of(zz * block, block), block))

    each_plane(take)
    each_plane(lambda zz: each(zz, own_tail.wait, lambda p: tail_to(p, p).wait_recv()))
    tall[...] = tail_in[...].astype(F32)
    for k in range(pick_count):
        for e in range(extra):
            got[base + e * peers:base + (e + 1) * peers, k * CAPT:(k + 1) * CAPT] = tall[
                :, e * pick_count + k, :
            ].astype(BF16)
    give(pl.ds(base, count))
    for k in range(pick_count):
        out_ref[:, k, :] = total[:, k * CAPT:(k + 1) * CAPT].astype(BF16)
    keep.wait()

    def sent(p):
        for move in (rows_to, picks_to, back_to, rest_to, tail_to):
            move(p, me).wait_send()

    each_plane(lambda zz: each(zz, lambda: None, sent))


def back_call(mixed, w_proj, images, slot_row, picks, captions, pick_count):
    tokens, width = images.shape
    peers = picks.shape[0]
    full_rows, extra = split_of(tokens, peers)
    slots = peers * (full_rows + extra)
    rest_shape = (peers, 8, -(-extra * (width // 128) // 8) * 128)
    tail_shape = (peers, -(-extra * pick_count // 8) * 8, CAPT)
    anywhere = pl.BlockSpec(memory_space=pl.ANY)
    far = pl.BlockSpec(memory_space=pltpu.HBM)
    full = pl.BlockSpec(memory_space=VMEM)
    dma = pltpu.SemaphoreType.DMA
    return pl.pallas_call(
        back_kernel,
        in_specs=[anywhere] * 2 + [far] + [full] * 2 + [far],
        out_specs=(anywhere, full),
        out_shape=(
            jax.ShapeDtypeStruct((tokens, width), BF16),
            jax.ShapeDtypeStruct((tokens, pick_count, CAPT), BF16),
        ),
        scratch_shapes=[
            VMEM(mixed.shape, BF16),
            VMEM(w_proj.shape, BF16),
            VMEM(images.shape, BF16),
            VMEM(captions.shape, BF16),
            dma((4,)),
            VMEM((slots, tokens), BF16),
            VMEM((slots, width), BF16),
            VMEM((slots, width), BF16),
            VMEM(picks.shape, BF16),
            VMEM((slots, pick_count * CAPT), BF16),
            VMEM((slots, pick_count * CAPT), BF16),
            VMEM((4 * full_rows, picks.shape[1]), F32),
            VMEM((peers * extra, picks.shape[1]), F32),
            VMEM((tokens, width), BF16),
            VMEM((tokens, pick_count * CAPT), F32),
            VMEM(rest_shape, F32),
            VMEM(rest_shape, BF16),
            VMEM(rest_shape, BF16),
            VMEM(tail_shape, F32),
            VMEM(tail_shape, BF16),
            VMEM(tail_shape, BF16),
        ]
        + [dma((peers,))] * 10
        + [dma((6,))],
        compiler_params=pltpu.CompilerParams(
            collective_id=1, has_side_effects=True, vmem_limit_bytes=BACK_LIMIT
        ),
        name="back",
    )(mixed, w_proj, images, slot_row, picks, captions)


def return_kernel(slot_ref, rows_ref, out_ref, *packed):
    if packed:
        (flat,) = packed
        flat[...] = jnp.zeros_like(flat)
        stride = flat.shape[0] // rows_ref.shape[0]
        for p in range(rows_ref.shape[0]):
            flat[p * stride:p * stride + rows_ref.shape[1], :] = rows_ref[p]
        rows = flat[...]
    else:
        rows = rows_ref[...]
    tokens, slots = out_ref.shape[0], rows.shape[0]
    pick = lax.broadcasted_iota(jnp.int32, (tokens, slots), 1) == slot_ref[...]
    onehot = jnp.where(pick, 1.0, 0.0).astype(BF16)
    got = jnp.dot(onehot, rows, preferred_element_type=F32).astype(BF16)
    for k in range(out_ref.shape[1]):
        out_ref[:, k, :] = got[:, k * CAPT:(k + 1) * CAPT]


def return_call(slot_col, rows, pick_count):
    full = pl.BlockSpec(memory_space=VMEM)
    return pl.pallas_call(
        return_kernel,
        in_specs=[full] * 2,
        out_specs=full,
        out_shape=jax.ShapeDtypeStruct((slot_col.shape[0], pick_count, CAPT), BF16),
        scratch_shapes=[pltpu.VMEM((rows.shape[0] * stride_of(rows.shape[1]), rows.shape[2]), BF16)]
        if rows.ndim == 3
        else [],
        compiler_params=pltpu.CompilerParams(vmem_limit_bytes=VLIMIT),
        name="give_back",
    )(slot_col, rows)


def local(
    images,
    norm_gain,
    qkv_values,
    qkv_exponents,
    proj_values,
    proj_exponents,
    captions,
    owners,
    candidates,
):
    token_count, width = images.shape
    peer_count = lax.axis_size("idx")
    me = lax.axis_index("idx")
    capacity = capacity_of(token_count, peer_count)

    pick_count = candidates.shape[1]
    gain = norm_gain[None, :]
    qkv_cols, proj_cols = qkv_values.shape[1], proj_values.shape[1]
    if fits(images, qkv_cols, proj_cols, qkv_exponents.shape[0], peer_count, lax.axis_size("rep")):
        mixed, w_proj, place, picks = front_call(
            images, norm_gain, qkv_values.T, proj_values.T, qkv_exponents, proj_exponents,
            owners.T, candidates.T, peer_count,
        )
        return back_call(
            mixed, w_proj.reshape(width, width), images, place, picks, captions, pick_count
        )

    def own_exponents(exponents, cols):
        return lax.dynamic_slice_in_dim(exponents, me * cols, cols, axis=1)

    qkv_own = dequant_rows(qkv_values, own_exponents(qkv_exponents, qkv_cols))
    proj_own = dequant_rows(proj_values, own_exponents(proj_exponents, proj_cols))
    owner_ids = owners[:, 0]
    onehot = (owner_ids[:, None] == jnp.arange(peer_count, dtype=jnp.int32)[None, :]).astype(
        jnp.int32
    )
    slot_rank = jnp.sum((jnp.cumsum(onehot, axis=0) - onehot) * onehot, axis=1)
    slot_index = owner_ids * capacity + slot_rank
    slots = peer_count * capacity
    dispatch = (jnp.arange(slots, dtype=jnp.int32)[:, None] == slot_index[None, :]).astype(BF16)
    send_picks = jnp.dot(dispatch, candidates.astype(BF16), preferred_element_type=F32).astype(BF16)
    w_qkv, w_proj = (lax.all_gather(own, "idx", axis=0, tiled=True) for own in (qkv_own, proj_own))
    qkv = qkv_call(images, gain, w_qkv)
    embedding, send_rows = attend_call(qkv, w_proj, images, slot_index[None, :], (slots,))

    def swap(blocks):
        shaped = blocks.reshape(peer_count, capacity, blocks.shape[1])
        moved = lax.all_to_all(shaped, "idx", split_axis=0, concat_axis=0, tiled=True)
        return moved.reshape(blocks.shape)

    returned = swap(score_call(swap(send_rows), swap(send_picks), captions))
    return (embedding, return_call(slot_index[:, None], returned, pick_count))


def solution(mesh):
    placed = (
        P(("rep", "idx"), None),
        P(),
        P(None, "idx"),
        P(),
        P(None, "idx"),
        P(),
        P(("rep", "idx"), None),
        P(("rep", "idx"), None),
        P(("rep", "idx"), None),
    )
    return jax.shard_map(
        local,
        mesh=mesh,
        in_specs=placed,
        out_specs=(P(("rep", "idx"), None), P(("rep", "idx"), None, None)),
        check_vma=False,
    )
```
